128 devices in a mesh: seq: 16 (over z_lo, y, core), head: 8 (over x, z_hi).
Axes of the slice: x: 4, y: 4, z: 4 (z_hi: 2, z_lo: 2; z = z_hi * 2 + z_lo), core: 2. Of those that a mesh axis runs over, the one named last changes fastest.
Arguments:
- frames: bfloat16 [8192, 2048], P('seq')
- w_query: bfloat16 [2048, 2048], P(None, 'head'), may hold values from -0.125 to 0.125
- w_key: bfloat16 [2048, 2048], P(None, 'head'), may hold values from -0.125 to 0.125
- w_value: bfloat16 [2048, 2048], P(None, 'head'), may hold values from -0.125 to 0.125
- w_out: bfloat16 [2048, 2048], P('head'), may hold values from -1 to 1
- conv_taps: float32 [31, 2048], P(None, 'head'), may hold values from -1 to 1
- conv_bias: float32 [2048], P('head'), may hold values from -1 to 1
- norm_gain: float32 [2048], replicated, may hold values from 0.5 to 1.5
- w_up: bfloat16 [2048, 8192], P(None, 'head'), may hold values from -0.125 to 0.125
- w_down: bfloat16 [8192, 2048], P('head'), may hold values from -0.0625 to 0.0625
- block_lists: int32 [64, 8], P('seq'), may hold values from 0 to 63, as said below
- block_counts: int32 [64], P('seq'), may hold values from 1 to 8, as said below
Outputs:
- layer_out: bfloat16 [8192, 2048], P('seq', 'head')
The draws below stay inside these ranges and needn't reach their ends.
Inputs may be any that keep to these rules, and one draw needn't show every extreme that they name: `block_lists`: entry 0 of query block b's list is b itself; the 8 entries of a list are distinct block indices. `block_counts`: query block 0 has all 8 entries active.
All inputs are finite; a program needn't handle non-finite values.
Results may differ from the reference program's by a relative error of at most 0.02.
The reference program's roundings to bfloat16 on the way count: a program that leaves them out, or rounds other values in their place, can miss the bound.
Values may be sent and summed in bfloat16 or wider, within the bound.
A program may use at most 128 MiB of HBM per device.

```python
import jax
import jax.numpy as jnp
from jax import lax

D = 2048
H = 32
HD = 64
FF = 8192
KERNEL = 31
BLK = 128
MAXACT = 8
F_DEV = 512
FRAMES = 8192
NBLK = 64
N_HEAD = 8


def draw_frames(key, part):
    first = jax.random.fold_in(key, 0)
    base = jax.random.normal(first, (FRAMES, D), jnp.float32)
    return jnp.clip(base, -40.0, 40.0).astype(jnp.bfloat16)


def active_blocks(key):
    inner = jax.random.fold_in(key, 17)
    list_key, count_key, level_key = jax.random.split(inner, 3)
    rows = jnp.arange(NBLK, dtype=jnp.int32)
    row_keys = jax.random.split(list_key, NBLK)

    def offsets_of(row_key):
        return jax.random.permutation(row_key, NBLK - 1)[:MAXACT - 1].astype(jnp.int32) + 1
    offsets = jax.vmap(offsets_of)(row_keys)
    offsets = jnp.concatenate([jnp.zeros((NBLK, 1), jnp.int32), offsets], axis=1)
    lists = (rows[:, None] + offsets) % NBLK
    shards = NBLK // (F_DEV // BLK)
    busy = jax.random.randint(level_key, (shards,), 0, 2)
    upper = jnp.where(busy[rows // (F_DEV // BLK)] == 1, MAXACT + 1, MAXACT // 2 + 1)
    counts = jax.random.randint(count_key, (NBLK,), 1, upper).astype(jnp.int32)
    counts = counts.at[0].set(MAXACT)
    return (lists.astype(jnp.int32), counts)


def draw_block_lists(key, part):
    return active_blocks(key)[0]


def draw_block_counts(key, part):
    return active_blocks(key)[1]


def levels(stream_key, shape, cuts, smallest, largest):
    def one(axis_at, blocks):
        steps = jax.random.uniform(jax.random.fold_in(jax.random.fold_in(stream_key, 6), axis_at), (blocks,), jnp.float32, smallest / len(cuts), largest / len(cuts))
        return jnp.repeat(jnp.exp(steps), shape[axis_at] // blocks).reshape((-1,) + (1,) * (len(shape) - axis_at - 1))

    factor_of = one(*cuts[0])
    for cut in cuts[1:]:
        factor_of = factor_of * one(*cut)
    return factor_of


def noise(rng, extent, scale, most, cuts=(), kind=jnp.bfloat16):
    gain = levels(rng, extent, cuts, -0.22, 0.18) if cuts else 1.0
    drawn = jax.random.normal(rng, extent, jnp.float32) * scale * gain
    return jnp.minimum(jnp.maximum(drawn, -most), most).astype(kind)


def setup_inputs(seed: int = 0) -> dict:
    key_list = jax.random.split(jax.random.key(seed), 13)
    return {
        "frames": draw_frames(jax.random.fold_in(key_list[12], 71), 0),
        "w_query": noise(key_list[1], (D, D), D ** -0.5, 0.125, ((1, 8),)),
        "w_key": noise(key_list[2], (D, D), D ** -0.5, 0.125, ((1, 8),)),
        "w_value": noise(key_list[3], (D, D), D ** -0.5, 0.125, ((1, 8),)),
        "w_out": noise(key_list[4], (D, D), 0.18, 1.0, ((0, 8),)),
        "conv_taps": noise(key_list[5], (KERNEL, D), 0.2, 1.0, ((1, 8),), jnp.float32),
        "conv_bias": jnp.clip(jax.random.uniform(key_list[6], (D,), jnp.float32, -1.0, 1.0) * levels(key_list[6], (D,), ((0, 8),), -0.4, 0.0), -1.0, 1.0),
        "norm_gain": jnp.clip(jax.random.uniform(key_list[7], (D,), jnp.float32, 0.5, 1.5), 0.5, 1.5),
        "w_up": noise(key_list[8], (D, FF), D ** -0.5, 0.125, ((1, 8),)),
        "w_down": noise(key_list[9], (FF, D), FF ** -0.5, 0.0625, ((0, 8),)),
        "block_lists": draw_block_lists(jax.random.fold_in(key_list[12], 71), 0),
        "block_counts": draw_block_counts(jax.random.fold_in(key_list[12], 71), 0),
    }


def reference(frames, w_query, w_key, w_value, w_out, conv_taps, conv_bias, norm_gain, w_up, w_down, block_lists, block_counts):
    total = frames.shape[0]
    query = jnp.dot(frames, w_query, preferred_element_type=jnp.float32).astype(jnp.bfloat16)
    keys = jnp.dot(frames, w_key, preferred_element_type=jnp.float32).astype(jnp.bfloat16)
    values = jnp.dot(frames, w_value, preferred_element_type=jnp.float32).astype(jnp.bfloat16)
    nblocks = total // BLK
    query_blocks = query.reshape(nblocks, BLK, H, HD)
    key_blocks = keys.reshape(nblocks, BLK, H, HD)
    value_blocks = values.reshape(nblocks, BLK, H, HD)
    slot_index = jnp.repeat(jnp.arange(MAXACT, dtype=jnp.int32), BLK)

    def one_block(item):
        query_part, listed, count = item
        key_sel = key_blocks[listed].reshape(MAXACT * BLK, H, HD).astype(jnp.float32)
        value_sel = value_blocks[listed].reshape(MAXACT * BLK, H, HD).astype(jnp.float32)
        live = slot_index < count
        scores = jnp.einsum('qhd,khd->hqk', query_part.astype(jnp.float32), key_sel) * 0.125
        scores = jnp.where(live[None, None, :], scores, -1e+30)
        top = lax.optimization_barrier(jnp.max(scores, axis=2, keepdims=True))
        probs = jnp.where(live[None, None, :], jnp.exp(scores - top), 0.0)
        total_w = lax.optimization_barrier(jnp.sum(probs, axis=2))
        rounded = lax.optimization_barrier(probs.astype(jnp.bfloat16)).astype(jnp.float32)
        out = jnp.einsum('hqk,khd->qhd', rounded, value_sel) / jnp.transpose(total_w)[:, :, None]
        return out.reshape(BLK, H * HD)
    attended = lax.map(one_block, (query_blocks, block_lists, block_counts))
    attended = attended.reshape(total, H * HD).astype(jnp.bfloat16)
    width = D // N_HEAD
    mixed = jnp.zeros((total, D), jnp.float32)
    for shard in range(N_HEAD):
        part = jnp.dot(attended[:, shard * width:(shard + 1) * width], w_out[shard * width:(shard + 1) * width], preferred_element_type=jnp.float32)
        mixed = mixed + lax.optimization_barrier(part.astype(jnp.bfloat16)).astype(jnp.float32)
    stream = (frames.astype(jnp.float32) + mixed).astype(jnp.bfloat16)
    half = KERNEL // 2
    padded = jnp.pad(stream.astype(jnp.float32), ((half, half), (0, 0)))
    conv_sum = jnp.zeros((total, D), jnp.float32)
    for tap in range(KERNEL):
        conv_sum = conv_sum + conv_taps[tap][None, :] * padded[tap:tap + total]
    second = (stream.astype(jnp.float32) + jax.nn.silu(conv_sum + conv_bias[None, :])).astype(jnp.bfloat16)
    whole = second.astype(jnp.float32)
    mean = lax.optimization_barrier(jnp.mean(whole, axis=1, keepdims=True))
    centered = whole - mean
    var = lax.optimization_barrier(jnp.mean(centered * centered, axis=1, keepdims=True))
    normed = (centered * lax.rsqrt(var + 1e-05) * norm_gain[None, :]).astype(jnp.bfloat16)
    ff_width = FF // N_HEAD
    ffsum = jnp.zeros((total, D), jnp.float32)
    for shard in range(N_HEAD):
        upper = jnp.dot(normed, w_up[:, shard * ff_width:(shard + 1) * ff_width], preferred_element_type=jnp.float32)
        hidden = jax.nn.silu(upper).astype(jnp.bfloat16)
        part = jnp.dot(hidden, w_down[shard * ff_width:(shard + 1) * ff_width], preferred_element_type=jnp.float32)
        ffsum = ffsum + lax.optimization_barrier(part.astype(jnp.bfloat16)).astype(jnp.float32)
    return (second.astype(jnp.float32) + ffsum).astype(jnp.bfloat16)
```

```python
import jax
import jax.numpy as jnp
from jax import lax
from jax.experimental import pallas as pl
from jax.experimental.pallas import tpu as pltpu
from jax.sharding import PartitionSpec as P

HD = 64
KERNEL = 31
NEG = -1e30


def qkv_kernel(x_ref, wq_ref, wk_ref, wv_ref, q_ref, kv_ref):
    width = wq_ref.shape[1]
    x = x_ref[...]
    q_ref[...] = jnp.dot(x, wq_ref[...], preferred_element_type=jnp.float32).astype(q_ref.dtype)
    kv_ref[:, :width] = jnp.dot(x, wk_ref[...], preferred_element_type=jnp.float32).astype(
        kv_ref.dtype
    )
    kv_ref[:, width:] = jnp.dot(x, wv_ref[...], preferred_element_type=jnp.float32).astype(
        kv_ref.dtype
    )


def project(frames, w_query, w_key, w_value):
    rows, depth = frames.shape
    width = w_query.shape[1]
    tile = 128
    weight = pl.BlockSpec((depth, width), lambda i: (0, 0), pipeline_mode=pl.Buffered(1))
    return pl.pallas_call(
        qkv_kernel,
        grid=(rows // tile,),
        in_specs=[pl.BlockSpec((tile, depth), lambda i: (i, 0)), weight, weight, weight],
        out_specs=[
            pl.BlockSpec((tile, width), lambda i: (i, 0)),
            pl.BlockSpec((tile, 2 * width), lambda i: (i, 0)),
        ],
        out_shape=[
            jax.ShapeDtypeStruct((rows, width), jnp.bfloat16),
            jax.ShapeDtypeStruct((rows, 2 * width), jnp.bfloat16),
        ],
        name="qkv",
    )(frames, w_query, w_key, w_value)


def attention_kernel(lists_ref, counts_ref, q_ref, kv_hbm, out_ref, kv_buf, sems):
    query_blocks, slots = lists_ref.shape
    block = q_ref.shape[0] // query_blocks
    width = q_ref.shape[1]
    copies = []
    for b in range(query_blocks):
        for j in range(slots):
            start = pl.multiple_of(lists_ref[b, j] * block, block)
            copy = pltpu.make_async_copy(
                kv_hbm.at[pl.ds(start, block), :],
                kv_buf.at[b, pl.ds(j * block, block), :],
                sems.at[b, j],
            )
            copy.start()
            copies.append(copy)
    lane = lax.broadcasted_iota(jnp.int32, (block, 2 * HD), 1)
    low = lane < HD
    slot_col = lax.broadcasted_iota(jnp.int32, (2 * block, slots * block), 1)
    for b in range(query_blocks):
        for j in range(slots):
            copies[b * slots + j].wait()
        live = slot_col < counts_ref[b] * block
        rows = pl.ds(b * block, block)
        for pair in range(width // (2 * HD)):
            cols = pl.ds(pair * 2 * HD, 2 * HD)
            q = q_ref[rows, cols]
            zero = jnp.zeros_like(q)
            both = jnp.concatenate([jnp.where(low, q, zero), jnp.where(low, zero, q)], axis=0)
            k = kv_buf[b, :, cols]
            v = kv_buf[b, :, pl.ds(width + pair * 2 * HD, 2 * HD)]
            scores = 0.125 * lax.dot_general(
                both, k, (((1,), (1,)), ((), ())), preferred_element_type=jnp.float32
            )
            scores = jnp.where(live, scores, NEG)
            top = jnp.max(scores, axis=1, keepdims=True)
            p = jnp.exp(scores - top)
            total = jnp.sum(p, axis=1, keepdims=True)
            o = jnp.dot(p.astype(jnp.bfloat16), v, preferred_element_type=jnp.float32) / total
            out_ref[rows, cols] = jnp.where(low, o[:block], o[block:]).astype(out_ref.dtype)


def attend(lists, counts, query, kv):
    rows, width = query.shape
    query_blocks, slots = lists.shape
    block = rows // query_blocks
    return pl.pallas_call(
        attention_kernel,
        in_specs=[
            pl.BlockSpec(memory_space=pltpu.SMEM),
            pl.BlockSpec(memory_space=pltpu.SMEM),
            pl.BlockSpec(memory_space=pltpu.VMEM),
            pl.BlockSpec(memory_space=pl.ANY),
        ],
        out_specs=pl.BlockSpec(memory_space=pltpu.VMEM),
        out_shape=jax.ShapeDtypeStruct((rows, width), jnp.bfloat16),
        scratch_shapes=[
            pltpu.VMEM((query_blocks, slots * block, 2 * width), jnp.bfloat16),
            pltpu.SemaphoreType.DMA((query_blocks, slots)),
        ],
        name="attend",
    )(lists, counts, query, kv)


def extended(cells, sides, width):
    for axis, dim in sides:
        count = lax.axis_size(axis)
        ends = count - 1
        head = lax.slice_in_dim(cells, 0, width, axis=dim)
        tail = lax.slice_in_dim(cells, cells.shape[dim] - width, cells.shape[dim], axis=dim)
        cells = jnp.concatenate(
            [
                lax.ppermute(tail, axis, [(i, (i + 1) % count) for i in range(ends)]),
                cells,
                lax.ppermute(head, axis, [((i + 1) % count, i) for i in range(ends)]),
            ],
            axis=dim,
        )
    return cells


def on_device(
    frames,
    w_query,
    w_key,
    w_value,
    w_out,
    conv_taps,
    conv_bias,
    norm_gain,
    w_up,
    w_down,
    block_lists,
    block_counts,
):
    frame_rows = frames.shape[0]
    width_dev = w_query.shape[1]
    query, own_kv = project(frames, w_query, w_key, w_value)
    kv = lax.all_gather(own_kv, "seq", axis=0, tiled=True)
    attended = attend(block_lists, block_counts, query, kv)
    columns = w_out
    mixed = lax.psum_scatter(
        jnp.einsum("fk,kc->cf", attended, columns, preferred_element_type=jnp.float32).astype(
            jnp.bfloat16
        ),
        "head",
        scatter_dimension=0,
        tiled=True,
    ).astype(jnp.float32)
    own_start = lax.axis_index("head") * width_dev
    residual_in = lax.dynamic_slice_in_dim(frames, own_start, width_dev, 1).T.astype(jnp.float32)
    stream = (residual_in + mixed).astype(jnp.bfloat16)
    padded = extended(stream, (("seq", 1),), KERNEL // 2).astype(jnp.float32)
    conv_sum = jnp.zeros((width_dev, frame_rows), jnp.float32)
    for tap in range(KERNEL):
        conv_sum = conv_sum + conv_taps[tap][:, None] * padded[:, tap : tap + frame_rows]
    second = (stream.astype(jnp.float32) + jax.nn.silu(conv_sum + conv_bias[:, None])).astype(
        jnp.bfloat16
    )
    whole = lax.all_gather(second, "head", axis=0, tiled=True).astype(jnp.float32)
    mean = jnp.mean(whole, axis=0, keepdims=True)
    centered = whole - mean
    var = jnp.mean(centered * centered, axis=0, keepdims=True)
    normed = (centered * lax.rsqrt(var + 1e-05) * norm_gain[:, None]).astype(jnp.bfloat16)
    upper = jnp.einsum("df,dk->fk", normed, w_up, preferred_element_type=jnp.float32)
    hidden = jax.nn.silu(upper).astype(jnp.bfloat16)
    columns = w_down
    ffsum = lax.psum_scatter(
        jnp.einsum("fk,kc->cf", hidden, columns, preferred_element_type=jnp.float32).astype(
            jnp.bfloat16
        ),
        "head",
        scatter_dimension=0,
        tiled=True,
    ).astype(jnp.float32)
    return (second.astype(jnp.float32) + ffsum).astype(jnp.bfloat16).T


def solution(mesh):
    placed = (
        P("seq", None),
        P(None, "head"),
        P(None, "head"),
        P(None, "head"),
        P("head", None),
        P(None, "head"),
        P("head"),
        P(),
        P(None, "head"),
        P("head", None),
        P("seq", None),
        P("seq"),
    )
    return jax.shard_map(
        on_device, mesh=mesh, in_specs=placed, out_specs=P("seq", "head"), check_vma=False
    )
```

```python
import functools

import jax
import jax.numpy as jnp
from jax import lax
from jax.experimental import pallas as pl
from jax.experimental.pallas import tpu as pltpu
from jax.sharding import PartitionSpec as P

HD = 64
KERNEL = 31
NEG = -1e30


def qkv_kernel(x_ref, wq_ref, wk_ref, wv_ref, q_ref, kv_ref):
    width = wq_ref.shape[1]
    x = x_ref[...]
    q_ref[...] = jnp.dot(x, wq_ref[...], preferred_element_type=jnp.float32).astype(q_ref.dtype)
    kv_ref[:, :width] = jnp.dot(x, wk_ref[...], preferred_element_type=jnp.float32).astype(
        kv_ref.dtype
    )
    kv_ref[:, width:] = jnp.dot(x, wv_ref[...], preferred_element_type=jnp.float32).astype(
        kv_ref.dtype
    )


def project(frames, w_query, w_key, w_value):
    rows, depth = frames.shape
    width = w_query.shape[1]
    tile = 128
    weight = pl.BlockSpec((depth, width), lambda i: (0, 0), pipeline_mode=pl.Buffered(1))
    return pl.pallas_call(
        qkv_kernel,
        grid=(rows // tile,),
        in_specs=[pl.BlockSpec((tile, depth), lambda i: (i, 0)), weight, weight, weight],
        out_specs=[
            pl.BlockSpec((tile, width), lambda i: (i, 0)),
            pl.BlockSpec((tile, 2 * width), lambda i: (i, 0)),
        ],
        out_shape=[
            jax.ShapeDtypeStruct((rows, width), jnp.bfloat16),
            jax.ShapeDtypeStruct((rows, 2 * width), jnp.bfloat16),
        ],
        name="qkv",
    )(frames, w_query, w_key, w_value)


def attention_kernel(lists_ref, counts_ref, q_ref, kv_hbm, out_ref, kv_buf, sems):
    query_blocks, slots = lists_ref.shape
    block = q_ref.shape[0] // query_blocks
    width = q_ref.shape[1]
    copies = []
    for b in range(query_blocks):
        for j in range(slots):
            start = pl.multiple_of(lists_ref[b, j] * block, block)
            copy = pltpu.make_async_copy(
                kv_hbm.at[pl.ds(start, block), :],
                kv_buf.at[b, pl.ds(j * block, block), :],
                sems.at[b, j],
            )
            copy.start()
            copies.append(copy)
    lane = lax.broadcasted_iota(jnp.int32, (block, 2 * HD), 1)
    low = lane < HD
    slot_col = lax.broadcasted_iota(jnp.int32, (2 * block, slots * block), 1)
    for b in range(query_blocks):
        for j in range(slots):
            copies[b * slots + j].wait()
        live = slot_col < counts_ref[b] * block
        rows = pl.ds(b * block, block)
        for pair in range(width // (2 * HD)):
            cols = pl.ds(pair * 2 * HD, 2 * HD)
            q = q_ref[rows, cols]
            zero = jnp.zeros_like(q)
            both = jnp.concatenate([jnp.where(low, q, zero), jnp.where(low, zero, q)], axis=0)
            k = kv_buf[b, :, cols]
            v = kv_buf[b, :, pl.ds(width + pair * 2 * HD, 2 * HD)]
            scores = 0.125 * lax.dot_general(
                both, k, (((1,), (1,)), ((), ())), preferred_element_type=jnp.float32
            )
            scores = jnp.where(live, scores, NEG)
            top = jnp.max(scores, axis=1, keepdims=True)
            p = jnp.exp(scores - top)
            total = jnp.sum(p, axis=1, keepdims=True)
            o = jnp.dot(p.astype(jnp.bfloat16), v, preferred_element_type=jnp.float32) / total
            out_ref[rows, cols] = jnp.where(low, o[:block], o[block:]).astype(out_ref.dtype)


def attend(lists, counts, query, kv):
    rows, width = query.shape
    query_blocks, slots = lists.shape
    block = rows // query_blocks
    return pl.pallas_call(
        attention_kernel,
        in_specs=[
            pl.BlockSpec(memory_space=pltpu.SMEM),
            pl.BlockSpec(memory_space=pltpu.SMEM),
            pl.BlockSpec(memory_space=pltpu.VMEM),
            pl.BlockSpec(memory_space=pl.ANY),
        ],
        out_specs=pl.BlockSpec(memory_space=pltpu.VMEM),
        out_shape=jax.ShapeDtypeStruct((rows, width), jnp.bfloat16),
        scratch_shapes=[
            pltpu.VMEM((query_blocks, slots * block, 2 * width), jnp.bfloat16),
            pltpu.SemaphoreType.DMA((query_blocks, slots)),
        ],
        name="attend",
    )(lists, counts, query, kv)


MESH = pl.DeviceIdType.MESH
PIECES = 4
HALO = 16


def silu(v):
    return v / (1.0 + jnp.exp(-v))


class Place:
    def __init__(self, heads, seqs):
        self.me = lax.axis_index("head")
        ring = heads // 2
        self.x = lax.div(self.me, 2)
        self.z = lax.rem(self.me, 2)
        self.x_right = lax.rem(self.x + 1, ring)
        self.x_left = lax.rem(self.x + ring - 1, ring)
        self.x_far = lax.rem(self.x + 2, ring)
        self.right = {"head": self.x_right * 2 + self.z}
        self.left = {"head": self.x_left * 2 + self.z}
        self.partner = {"head": self.x * 2 + 1 - self.z}
        self.s = lax.axis_index("seq")
        self.after = {"seq": lax.rem(self.s + 1, seqs)}
        self.before = {"seq": lax.rem(self.s + seqs - 1, seqs)}

    def greet(self):
        barrier = pltpu.get_barrier_semaphore()
        others = (self.right, self.left, self.partner, self.after, self.before)
        for other in others:
            pl.semaphore_signal(barrier, inc=1, device_id=other, device_id_type=MESH)
        pl.semaphore_wait(barrier, len(others))

    def ways(self, p):
        if p < PIECES // 2:
            return self.right, self.left, self.x_right, self.x_left
        return self.left, self.right, self.x_left, self.x_right


def send(src, dst, sems, key, device):
    copy = pltpu.make_async_remote_copy(
        src_ref=src,
        dst_ref=dst,
        send_sem=sems.at[0, key],
        recv_sem=sems.at[1, key],
        device_id=device,
        device_id_type=MESH,
    )
    copy.start()
    return copy


class Scatter:
    def __init__(self, place, a, w, bufs, sems):
        self.place, self.a, self.w = place, a, w
        (self.relay, self.direct, self.sums, self.zbuf, self.acc) = bufs
        self.sems = sems
        self.rows = a.shape[0] // PIECES
        self.width = w.shape[1] // 4
        self.copies = {}

    def part(self, p, xd):
        cols = pl.ds(pl.multiple_of(xd * self.width, self.width), self.width)
        return jnp.dot(
            self.a[p * self.rows : (p + 1) * self.rows, :],
            self.w[:, cols],
            preferred_element_type=jnp.float32,
        )

    def go(self, p, kind, buf, device):
        self.copies[p, kind] = send(
            buf.at[0, p], buf.at[1, p], self.sems, p * 4 + kind, device
        )

    def first(self, p):
        fwd, bwd, x_fwd, x_bwd = self.place.ways(p)
        self.relay[0, p] = self.part(p, self.place.x_far).astype(jnp.bfloat16)
        self.go(p, 0, self.relay, fwd)
        self.direct[0, p] = self.part(p, x_bwd).astype(jnp.bfloat16)
        self.go(p, 1, self.direct, bwd)

    def second(self, p):
        fwd, bwd, x_fwd, x_bwd = self.place.ways(p)
        mine = self.part(p, x_fwd)
        self.copies[p, 0].wait_recv()
        self.sums[0, p] = (mine + self.relay[1, p].astype(jnp.float32)).astype(jnp.bfloat16)
        self.go(p, 2, self.sums, fwd)

    def own(self, p):
        self.acc[p] = self.part(p, self.place.x)

    def third(self, p):
        self.copies[p, 1].wait_recv()
        self.copies[p, 2].wait_recv()
        self.acc[p] = (
            self.acc[p]
            + self.direct[1, p].astype(jnp.float32)
            + self.sums[1, p].astype(jnp.float32)
        )
        half = self.width // 2
        other = pl.ds(pl.multiple_of((1 - self.place.z) * half, half), half)
        self.zbuf[0, p] = self.acc[p, :, other].astype(jnp.bfloat16)
        self.go(p, 3, self.zbuf, self.place.partner)

    def last(self, p):
        self.copies[p, 3].wait_recv()
        half = self.width // 2
        kept = pl.ds(pl.multiple_of(self.place.z * half, half), half)
        return self.acc[p, :, kept] + self.zbuf[1, p].astype(jnp.float32)

    def finish(self):
        for copy in self.copies.values():
            copy.wait_send()


class Gather:
    def __init__(self, place, whole, sems):
        self.place, self.whole, self.sems = place, whole, sems
        self.rows = whole.shape[0] // PIECES
        self.width = whole.shape[1] // 8
        self.copies = {}

    def view(self, p, head, count):
        width = self.width
        cols = pl.ds(pl.multiple_of(head * width, width), count * width)
        return self.whole.at[p * self.rows : (p + 1) * self.rows, cols]

    def go(self, p, kind, head, count, device):
        view = self.view(p, head, count)
        self.copies[p, kind] = send(view, view, self.sems, p * 6 + kind, device)

    def first(self, p):
        fwd, bwd, x_fwd, x_bwd = self.place.ways(p)
        self.go(p, 0, self.place.me, 1, self.place.partner)
        self.go(p, 1, self.place.me, 1, fwd)
        self.go(p, 2, self.place.me, 1, bwd)

    def second(self, p):
        fwd, bwd, x_fwd, x_bwd = self.place.ways(p)
        self.copies[p, 0].wait_recv()
        mate = self.place.x * 2 + 1 - self.place.z
        self.go(p, 3, mate, 1, fwd)
        self.go(p, 4, mate, 1, bwd)

    def third(self, p):
        fwd, bwd, x_fwd, x_bwd = self.place.ways(p)
        self.copies[p, 1].wait_recv()
        self.copies[p, 3].wait_recv()
        self.go(p, 5, x_bwd * 2, 2, fwd)

    def last(self, p):
        self.copies[p, 2].wait_recv()
        self.copies[p, 4].wait_recv()
        self.copies[p, 5].wait_recv()

    def finish(self):
        for copy in self.copies.values():
            copy.wait_send()


def tail_kernel(
    heads,
    seqs,
    att_ref,
    w_out_ref,
    frames_hbm,
    taps_ref,
    bias_ref,
    gain_ref,
    up_hbm,
    down_hbm,
    out_ref,
    up,
    down,
    resid,
    stream,
    halo,
    pad,
    second,
    whole,
    hidden,
    relay_o,
    direct_o,
    sums_o,
    z_o,
    acc_o,
    relay_f,
    direct_f,
    sums_f,
    z_f,
    acc_f,
    local_sems,
    sems_o,
    sems_h,
    sems_g,
    sems_f,
):
    place = Place(heads, seqs)
    frame_rows, width = out_ref.shape
    rows = frame_rows // PIECES
    own_cols = pl.ds(pl.multiple_of(place.me * width, width), width)
    get_resid = pltpu.make_async_copy(frames_hbm.at[:, own_cols], resid, local_sems.at[0])
    get_up = pltpu.make_async_copy(up_hbm, up, local_sems.at[1])
    get_down = pltpu.make_async_copy(down_hbm, down, local_sems.at[2])
    get_resid.start()
    get_up.start()
    get_down.start()
    place.greet()

    outer, inner = (0, PIECES - 1), tuple(range(1, PIECES - 1))
    mix = Scatter(place, att_ref, w_out_ref, (relay_o, direct_o, sums_o, z_o, acc_o), sems_o)
    for p in outer:
        mix.first(p)
    for p in outer:
        mix.second(p)
    for p in inner:
        mix.first(p)
    for p in outer + inner:
        mix.own(p)
    for p in inner:
        mix.second(p)
    for p in outer:
        mix.third(p)
    get_resid.wait()

    def place_stream(p):
        at = slice(p * rows, (p + 1) * rows)
        value = (resid[at, :].astype(jnp.float32) + mix.last(p)).astype(jnp.bfloat16)
        stream[at, :] = value
        pad[HALO + p * rows : HALO + (p + 1) * rows, :] = value.astype(jnp.float32)

    for p in outer:
        place_stream(p)
    to_before = send(stream.at[0:HALO, :], halo.at[1], sems_h, 0, place.before)
    to_after = send(
        stream.at[frame_rows - HALO : frame_rows, :], halo.at[0], sems_h, 1, place.after
    )
    for p in inner:
        mix.third(p)
    for p in inner:
        place_stream(p)
    to_before.wait_recv()
    to_after.wait_recv()
    top = jnp.where(place.s == 0, 0.0, 1.0)
    bottom = jnp.where(place.s == seqs - 1, 0.0, 1.0)
    pad[0:HALO, :] = halo[0].astype(jnp.float32) * top
    pad[HALO + frame_rows : 2 * HALO + frame_rows, :] = halo[1].astype(jnp.float32) * bottom

    ring = Gather(place, whole, sems_g)
    order = (0, PIECES - 1) + tuple(range(1, PIECES - 1))

    def convolve(p):
        shift = HALO - KERNEL // 2
        total = jnp.zeros((rows, width), jnp.float32)
        for tap in range(KERNEL):
            total = total + taps_ref[tap : tap + 1, :] * pad[
                pl.ds(p * rows + tap + shift, rows), :
            ]
        at = slice(p * rows, (p + 1) * rows)
        value = pad[HALO + p * rows : HALO + (p + 1) * rows, :] + silu(total + bias_ref[...])
        value = value.astype(jnp.bfloat16)
        second[at, :] = value
        whole[at, own_cols] = value

    def feed(p):
        at = slice(p * rows, (p + 1) * rows)
        cells = whole[at, :].astype(jnp.float32)
        mean = jnp.mean(cells, axis=1, keepdims=True)
        centered = cells - mean
        var = jnp.mean(centered * centered, axis=1, keepdims=True)
        normed = (centered * lax.rsqrt(var + 1e-05) * gain_ref[...]).astype(jnp.bfloat16)
        upper = jnp.dot(normed, up[...], preferred_element_type=jnp.float32)
        hidden[at, :] = silu(upper).astype(jnp.bfloat16)

    for p in order:
        convolve(p)
        ring.first(p)
    for p in order:
        ring.second(p)
    for p in order[:2]:
        ring.third(p)
    get_up.wait()
    get_down.wait()
    ffn = Scatter(place, hidden, down, (relay_f, direct_f, sums_f, z_f, acc_f), sems_f)
    for i, p in enumerate(order):
        if i + 2 < PIECES:
            ring.third(order[i + 2])
        ring.last(p)
        feed(p)
        ffn.first(p)
        if i >= 1:
            ffn.second(order[i - 1])
        ffn.own(p)
        if i >= 2:
            ffn.third(order[i - 2])
    ffn.second(order[-1])
    for p in order[-2:]:
        ffn.third(p)
    for p in order:
        at = slice(p * rows, (p + 1) * rows)
        out_ref[at, :] = (second[at, :].astype(jnp.float32) + ffn.last(p)).astype(out_ref.dtype)
    mix.finish()
    to_before.wait_send()
    to_after.wait_send()
    ring.finish()
    ffn.finish()


def tail(attended, w_out, frames, taps, bias, gain, w_up, w_down):
    frame_rows, width = attended.shape
    depth = frames.shape[1]
    hidden = w_up.shape[1]
    rows = frame_rows // PIECES
    vmem = pl.BlockSpec(memory_space=pltpu.VMEM)
    hbm = pl.BlockSpec(memory_space=pl.ANY)
    bf16, f32 = jnp.bfloat16, jnp.float32
    quarter = depth // 4
    buffers = [pltpu.VMEM((2, PIECES, rows, quarter), bf16)] * 3 + [
        pltpu.VMEM((2, PIECES, rows, width), bf16),
        pltpu.VMEM((PIECES, rows, quarter), f32),
    ]
    dma = pltpu.SemaphoreType.DMA
    return pl.pallas_call(
        functools.partial(tail_kernel, lax.axis_size("head"), lax.axis_size("seq")),
        in_specs=[vmem, vmem, hbm, vmem, vmem, vmem, hbm, hbm],
        out_specs=vmem,
        out_shape=jax.ShapeDtypeStruct((frame_rows, width), bf16),
        scratch_shapes=[
            pltpu.VMEM((depth, hidden), bf16),
            pltpu.VMEM((hidden, depth), bf16),
            pltpu.VMEM((frame_rows, width), bf16),
            pltpu.VMEM((frame_rows, width), bf16),
            pltpu.VMEM((2, HALO, width), bf16),
            pltpu.VMEM((frame_rows + 2 * HALO, width), f32),
            pltpu.VMEM((frame_rows, width), bf16),
            pltpu.VMEM((frame_rows, depth), bf16),
            pltpu.VMEM((frame_rows, hidden), bf16),
        ]
        + buffers
        + buffers
        + [
            dma((3,)),
            dma((2, PIECES * 4)),
            dma((2, 2)),
            dma((2, PIECES * 6)),
            dma((2, PIECES * 4)),
        ],
        compiler_params=pltpu.CompilerParams(
            collective_id=0, has_side_effects=True, vmem_limit_bytes=60 * 1024 * 1024
        ),
        name="tail",
    )(attended, w_out, frames, taps, bias[None, :], gain[None, :], w_up, w_down)


def on_device(
    frames,
    w_query,
    w_key,
    w_value,
    w_out,
    conv_taps,
    conv_bias,
    norm_gain,
    w_up,
    w_down,
    block_lists,
    block_counts,
):
    query, own_kv = project(frames, w_query, w_key, w_value)
    kv = lax.all_gather(own_kv, "seq", axis=0, tiled=True)
    attended = attend(block_lists, block_counts, query, kv)
    return tail(attended, w_out, frames, conv_taps, conv_bias, norm_gain, w_up, w_down)


def solution(mesh):
    placed = (
        P("seq", None),
        P(None, "head"),
        P(None, "head"),
        P(None, "head"),
        P("head", None),
        P(None, "head"),
        P("head"),
        P(),
        P(None, "head"),
        P("head", None),
        P("seq", None),
        P("seq"),
    )
    return jax.shard_map(
        on_device, mesh=mesh, in_specs=placed, out_specs=P("seq", "head"), check_vma=False
    )
```

```python
import functools

import jax
import jax.numpy as jnp
from jax import lax
from jax.experimental import pallas as pl
from jax.experimental.pallas import tpu as pltpu
from jax.sharding import PartitionSpec as P

HD = 64
KERNEL = 31
NEG = -1e30


MESH = pl.DeviceIdType.MESH
PIECES = 4
HALO = 16
YS = 4
BLOCK = 128
SLOTS = 8
COUNT_ROW = 4


def silu(v):
    return v / (1.0 + jnp.exp(-v))


class Place:
    def __init__(self, heads, seqs):
        self.me = lax.axis_index("head")
        ring = heads // 2
        self.x = lax.div(self.me, 2)
        self.z = lax.rem(self.me, 2)
        self.x_right = lax.rem(self.x + 1, ring)
        self.x_left = lax.rem(self.x + ring - 1, ring)
        self.x_far = lax.rem(self.x + 2, ring)
        self.right = {"head": self.x_right * 2 + self.z}
        self.left = {"head": self.x_left * 2 + self.z}
        self.partner = {"head": self.x * 2 + 1 - self.z}
        self.s = lax.axis_index("seq")
        self.core = lax.rem(self.s, 2)
        self.y = lax.rem(lax.div(self.s, 2), YS)
        self.zl = lax.div(self.s, 2 * YS)
        self.after = {"seq": lax.rem(self.s + 1, seqs)}
        self.before = {"seq": lax.rem(self.s + seqs - 1, seqs)}

    def greet(self):
        barrier = pltpu.get_barrier_semaphore()
        others = [self.right, self.left, self.partner, self.after, self.before]
        others += [self.far(d) for d in range(1, YS)]
        for other in others:
            pl.semaphore_signal(barrier, inc=1, device_id=other, device_id_type=MESH)
        pl.semaphore_wait(barrier, len(others))

    def seq_of(self, z_at, y_at, core_at):
        return (z_at * YS + y_at) * 2 + core_at

    def far(self, d):
        return {"seq": self.seq_of(self.zl, lax.rem(self.y + d, YS), self.core)}

    def ways(self, p):
        if p < PIECES // 2:
            return self.right, self.left, self.x_right, self.x_left
        return self.left, self.right, self.x_left, self.x_right


def send(src, dst, sems, key, device):
    copy = pltpu.make_async_remote_copy(
        src_ref=src,
        dst_ref=dst,
        send_sem=sems.at[0, key],
        recv_sem=sems.at[1, key],
        device_id=device,
        device_id_type=MESH,
    )
    copy.start()
    return copy


def swap(value):
    return pltpu.roll(value, HD, 1)


def front_kernel(
    frames_hbm,
    wq_hbm,
    wk_hbm,
    wv_hbm,
    lists_ref,
    counts_ref,
    kv_all,
    q_all,
    tables,
    table,
    x,
    wq,
    wk,
    wv,
    kv_out,
    q_out,
    local_sems,
    sems,
):
    frame_rows = x.shape[0]
    half = frame_rows // 2
    f32, bf16 = jnp.float32, jnp.bfloat16
    loads = []
    for i, (src, dst) in enumerate(
        ((frames_hbm, x), (wk_hbm, wk), (wv_hbm, wv), (wq_hbm, wq))
    ):
        load = pltpu.make_async_copy(src, dst, local_sems.at[i])
        load.start()
        loads.append(load)

    table[...] = jnp.zeros_like(table)
    table[: lists_ref.shape[0], : lists_ref.shape[1]] = lists_ref[...]
    table[COUNT_ROW : COUNT_ROW + 1, : counts_ref.shape[1]] = counts_ref[...]

    s = lax.axis_index("seq")
    core = lax.rem(s, 2)
    y = lax.rem(lax.div(s, 2), YS)
    zl = lax.div(s, 2 * YS)

    def seq_of(z_at, y_at, core_at):
        return (z_at * YS + y_at) * 2 + core_at

    def far(d):
        return {"seq": seq_of(zl, lax.rem(y + d, YS), core)}

    mate = {"seq": seq_of(zl, y, 1 - core)}
    across = {"seq": seq_of(1 - zl, y, core)}
    barrier = pltpu.get_barrier_semaphore()
    others = [far(d) for d in range(1, YS)] + [mate, across]
    for other in others:
        pl.semaphore_signal(barrier, inc=1, device_id=other, device_id_type=MESH)

    low = lax.broadcasted_iota(jnp.int32, (half, 2 * HD), 1) < HD
    for load in loads[:3]:
        load.wait()
    for part in range(2):
        rows = slice(part * half, (part + 1) * half)
        k = jnp.dot(x[rows, :], wk[...], preferred_element_type=f32)
        v = jnp.dot(x[rows, :], wv[...], preferred_element_type=f32)
        for pair in range(YS // 2):
            cols = slice(pair * 2 * HD, (pair + 1) * 2 * HD)
            kp, vp = k[:, cols], v[:, cols]
            kv_out[2 * pair, rows, :] = jnp.where(low, kp, swap(vp)).astype(bf16)
            kv_out[2 * pair + 1, rows, :] = jnp.where(low, swap(kp), vp).astype(bf16)
    pl.semaphore_wait(barrier, len(others))

    def rows_of(z_at, y_at, core_at):
        start = seq_of(z_at, y_at, core_at) * frame_rows
        return kv_all.at[pl.ds(pl.multiple_of(start, frame_rows), frame_rows), :]

    sent = {}
    here = rows_of(zl, y, core)
    for d in (2, 1, 3):
        to = lax.rem(y + d, YS)
        sent["kv", d] = send(kv_out.at[to], here, sems, d, far(d))
        sent["table", d] = send(table, tables.at[y], sems, 4 + d, far(d))
    sent["across", 0] = send(kv_out.at[y], here, sems, 8, across)
    sent["mate", 0] = send(kv_out.at[y], here, sems, 12, mate)
    keep = [
        pltpu.make_async_copy(kv_out.at[y], here, local_sems.at[4]),
        pltpu.make_async_copy(table, tables.at[y], local_sems.at[5]),
    ]
    for copy in keep:
        copy.start()

    loads[3].wait()
    q = 0.125 * jnp.dot(x[...], wq[...], preferred_element_type=f32)
    for pair in range(YS // 2):
        cols = slice(pair * 2 * HD, (pair + 1) * 2 * HD)
        top, bottom = q[:half, cols], q[half:, cols]
        q_out[2 * pair] = jnp.where(low, top, swap(bottom)).astype(bf16)
        q_out[2 * pair + 1] = jnp.where(low, swap(top), bottom).astype(bf16)
    for d in (2, 1, 3):
        to = lax.rem(y + d, YS)
        sent["q", d] = send(q_out.at[to], q_all.at[y], sems, 20 + d, far(d))
    keep.append(pltpu.make_async_copy(q_out.at[y], q_all.at[y], local_sems.at[6]))
    keep[-1].start()

    for d in (1, 3, 2):
        sent["kv", d].wait_recv()
        piece = rows_of(zl, lax.rem(y + YS - d, YS), core)
        sent["across", d] = send(piece, piece, sems, 8 + d, across)
        sent["mate", d] = send(piece, piece, sems, 12 + d, mate)
    for d in (0, 1, 3, 2):
        sent["across", d].wait_recv()
        piece = rows_of(1 - zl, lax.rem(y + YS - d, YS), core)
        sent["over", d] = send(piece, piece, sems, 16 + d, mate)
    for d in range(1, YS):
        sent["table", d].wait_recv()
    for d in range(1, YS):
        sent["q", d].wait_recv()
    for d in range(YS):
        sent["mate", d].wait_recv()
    for d in range(YS):
        sent["over", d].wait_recv()
    for copy in keep:
        copy.wait()
    for copy in sent.values():
        copy.wait_send()


def attention_kernel(tables_ref, q_ref, kv_ref, out_ref):
    f32, bf16 = jnp.float32, jnp.bfloat16
    sources, half, lanes = q_ref.shape
    block, slots = BLOCK, SLOTS
    per_half = half // block
    low = lax.broadcasted_iota(jnp.int32, (block, lanes), 1) < HD
    slot_col = lax.broadcasted_iota(jnp.int32, (block, slots * block), 1)

    def attend(source, b):
        packed = q_ref[source, (b % per_half) * block : (b % per_half + 1) * block, :]
        packed = packed.astype(f32)
        if b >= per_half:
            packed = swap(packed)
        query = jnp.where(low, packed, 0.0).astype(bf16)
        cells = []
        for j in range(slots):
            start = pl.multiple_of(tables_ref[source, b, j] * block, block)
            cells.append(kv_ref[pl.ds(start, block), :])
        kv = jnp.concatenate(cells, axis=0)
        scores = lax.dot_general(query, kv, (((1,), (1,)), ((), ())), preferred_element_type=f32)
        live = slot_col < tables_ref[source, COUNT_ROW, b] * block
        scores = jnp.where(live, scores, NEG)
        top = jnp.max(scores, axis=1, keepdims=True)
        p = jnp.exp(scores - top)
        total = jnp.sum(p, axis=1, keepdims=True)
        return jnp.dot(p.astype(bf16), kv, preferred_element_type=f32) / total

    for source in range(sources):
        for b in range(per_half):
            early, late = attend(source, b), attend(source, b + per_half)
            rows = slice(b * block, (b + 1) * block)
            out_ref[source, rows, :] = jnp.where(low, swap(early), late).astype(bf16)


def attend_listed(tables, q_all, kv_all):
    vmem = pl.BlockSpec(memory_space=pltpu.VMEM)
    return pl.pallas_call(
        attention_kernel,
        in_specs=[pl.BlockSpec(memory_space=pltpu.SMEM), vmem, vmem],
        out_specs=vmem,
        out_shape=jax.ShapeDtypeStruct(q_all.shape, jnp.bfloat16),
        compiler_params=pltpu.CompilerParams(vmem_limit_bytes=32 * 1024 * 1024),
        name="attend",
    )(tables, q_all, kv_all)


def front(frames, w_query, w_key, w_value, lists, counts):
    frame_rows, depth = frames.shape
    width = w_query.shape[1]
    seqs = lax.axis_size("seq")
    bf16 = jnp.bfloat16
    hbm = pl.BlockSpec(memory_space=pltpu.HBM)
    free = pl.BlockSpec(memory_space=pl.ANY)
    vmem = pl.BlockSpec(memory_space=pltpu.VMEM)
    dma = pltpu.SemaphoreType.DMA
    lanes = 2 * HD
    return pl.pallas_call(
        front_kernel,
        in_specs=[hbm, hbm, hbm, hbm, vmem, vmem],
        out_specs=[free, free, free],
        out_shape=[
            jax.ShapeDtypeStruct((seqs * frame_rows, lanes), bf16),
            jax.ShapeDtypeStruct((YS, frame_rows // 2, lanes), bf16),
            jax.ShapeDtypeStruct((YS, 8, 128), jnp.int32),
        ],
        scratch_shapes=[
            pltpu.VMEM((8, 128), jnp.int32),
            pltpu.VMEM((frame_rows, depth), bf16),
            pltpu.VMEM((depth, width), bf16),
            pltpu.VMEM((depth, width), bf16),
            pltpu.VMEM((depth, width), bf16),
            pltpu.VMEM((YS, frame_rows, lanes), bf16),
            pltpu.VMEM((YS, frame_rows // 2, lanes), bf16),
            dma((7,)),
            dma((2, 24)),
        ],
        compiler_params=pltpu.CompilerParams(
            collective_id=1, has_side_effects=True, vmem_limit_bytes=48 * 1024 * 1024
        ),
        name="front",
    )(frames, w_query, w_key, w_value, lists, counts[None, :])


class Scatter:
    def __init__(self, place, a, w, bufs, sems):
        self.place, self.a, self.w = place, a, w
        (self.relay, self.direct, self.sums, self.zbuf, self.acc) = bufs
        self.sems = sems
        self.rows = a.shape[0] // PIECES
        self.width = w.shape[1] // 4
        self.copies = {}

    def part(self, p, xd):
        cols = pl.ds(pl.multiple_of(xd * self.width, self.width), self.width)
        return jnp.dot(
            self.a[p * self.rows : (p + 1) * self.rows, :],
            self.w[:, cols],
            preferred_element_type=jnp.float32,
        )

    def go(self, p, kind, buf, device):
        self.copies[p, kind] = send(
            buf.at[0, p], buf.at[1, p], self.sems, p * 4 + kind, device
        )

    def first(self, p):
        fwd, bwd, x_fwd, x_bwd = self.place.ways(p)
        self.relay[0, p] = self.part(p, self.place.x_far).astype(jnp.bfloat16)
        self.go(p, 0, self.relay, fwd)
        self.direct[0, p] = self.part(p, x_bwd).astype(jnp.bfloat16)
        self.go(p, 1, self.direct, bwd)

    def second(self, p):
        fwd, bwd, x_fwd, x_bwd = self.place.ways(p)
        mine = self.part(p, x_fwd)
        self.copies[p, 0].wait_recv()
        self.sums[0, p] = (mine + self.relay[1, p].astype(jnp.float32)).astype(jnp.bfloat16)
        self.go(p, 2, self.sums, fwd)

    def own(self, p):
        self.acc[p] = self.part(p, self.place.x)

    def third(self, p):
        self.copies[p, 1].wait_recv()
        self.copies[p, 2].wait_recv()
        self.acc[p] = (
            self.acc[p]
            + self.direct[1, p].astype(jnp.float32)
            + self.sums[1, p].astype(jnp.float32)
        )
        half = self.width // 2
        other = pl.ds(pl.multiple_of((1 - self.place.z) * half, half), half)
        self.zbuf[0, p] = self.acc[p, :, other].astype(jnp.bfloat16)
        self.go(p, 3, self.zbuf, self.place.partner)

    def last(self, p):
        self.copies[p, 3].wait_recv()
        half = self.width // 2
        kept = pl.ds(pl.multiple_of(self.place.z * half, half), half)
        return self.acc[p, :, kept] + self.zbuf[1, p].astype(jnp.float32)

    def finish(self):
        for copy in self.copies.values():
            copy.wait_send()


class Gather:
    def __init__(self, place, whole, sems):
        self.place, self.whole, self.sems = place, whole, sems
        self.rows = whole.shape[0] // PIECES
        self.width = whole.shape[1] // 8
        self.copies = {}

    def view(self, p, head, count):
        width = self.width
        cols = pl.ds(pl.multiple_of(head * width, width), count * width)
        return self.whole.at[p * self.rows : (p + 1) * self.rows, cols]

    def go(self, p, kind, head, count, device):
        view = self.view(p, head, count)
        self.copies[p, kind] = send(view, view, self.sems, p * 6 + kind, device)

    def first(self, p):
        fwd, bwd, x_fwd, x_bwd = self.place.ways(p)
        self.go(p, 0, self.place.me, 1, self.place.partner)
        self.go(p, 1, self.place.me, 1, fwd)
        self.go(p, 2, self.place.me, 1, bwd)

    def second(self, p):
        fwd, bwd, x_fwd, x_bwd = self.place.ways(p)
        self.copies[p, 0].wait_recv()
        mate = self.place.x * 2 + 1 - self.place.z
        self.go(p, 3, mate, 1, fwd)
        self.go(p, 4, mate, 1, bwd)

    def third(self, p):
        fwd, bwd, x_fwd, x_bwd = self.place.ways(p)
        self.copies[p, 1].wait_recv()
        self.copies[p, 3].wait_recv()
        self.go(p, 5, x_bwd * 2, 2, fwd)

    def last(self, p):
        self.copies[p, 2].wait_recv()
        self.copies[p, 4].wait_recv()
        self.copies[p, 5].wait_recv()

    def finish(self):
        for copy in self.copies.values():
            copy.wait_send()


def tail_kernel(
    heads,
    seqs,
    att_ref,
    w_out_hbm,
    frames_hbm,
    taps_ref,
    bias_ref,
    gain_ref,
    up_hbm,
    down_hbm,
    out_ref,
    w_out,
    up,
    down,
    resid,
    stream,
    halo,
    pad,
    second,
    whole,
    hidden,
    relay_o,
    direct_o,
    sums_o,
    z_o,
    acc_o,
    relay_f,
    direct_f,
    sums_f,
    z_f,
    acc_f,
    ret_in,
    attended,
    local_sems,
    sems_r,
    sems_o,
    sems_h,
    sems_g,
    sems_f,
):
    place = Place(heads, seqs)
    frame_rows, width = out_ref.shape
    rows = frame_rows // PIECES
    own_cols = pl.ds(pl.multiple_of(place.me * width, width), width)
    get_resid = pltpu.make_async_copy(frames_hbm.at[:, own_cols], resid, local_sems.at[0])
    get_up = pltpu.make_async_copy(up_hbm, up, local_sems.at[1])
    get_down = pltpu.make_async_copy(down_hbm, down, local_sems.at[2])
    get_out = pltpu.make_async_copy(w_out_hbm, w_out, local_sems.at[4])
    get_out.start()
    get_resid.start()
    get_up.start()
    get_down.start()
    place.greet()

    back = [
        send(att_ref.at[lax.rem(place.y + d, YS)], ret_in.at[place.y], sems_r, d, place.far(d))
        for d in (2, 1, 3)
    ]
    own_back = pltpu.make_async_copy(
        att_ref.at[place.y], ret_in.at[place.y], local_sems.at[3]
    )
    own_back.start()
    half = frame_rows // 2
    low = lax.broadcasted_iota(jnp.int32, (half, 2 * HD), 1) < HD
    own_back.wait()
    for copy in back:
        copy.wait_recv()
    for pair in range(YS // 2):
        cols = slice(pair * 2 * HD, (pair + 1) * 2 * HD)
        one, two = ret_in[2 * pair].astype(jnp.float32), ret_in[2 * pair + 1].astype(jnp.float32)
        attended[:half, cols] = jnp.where(low, one, swap(two)).astype(jnp.bfloat16)
        attended[half:, cols] = jnp.where(low, swap(one), two).astype(jnp.bfloat16)

    outer, inner = (0, PIECES - 1), tuple(range(1, PIECES - 1))
    get_out.wait()
    mix = Scatter(place, attended, w_out, (relay_o, direct_o, sums_o, z_o, acc_o), sems_o)
    for p in outer:
        mix.first(p)
    for p in outer:
        mix.second(p)
    for p in inner:
        mix.first(p)
    for p in outer + inner:
        mix.own(p)
    for p in inner:
        mix.second(p)
    for p in outer:
        mix.third(p)
    get_resid.wait()

    def place_stream(p):
        at = slice(p * rows, (p + 1) * rows)
        value = (resid[at, :].astype(jnp.float32) + mix.last(p)).astype(jnp.bfloat16)
        stream[at, :] = value
        pad[HALO + p * rows : HALO + (p + 1) * rows, :] = value.astype(jnp.float32)

    for p in outer:
        place_stream(p)
    to_before = send(stream.at[0:HALO, :], halo.at[1], sems_h, 0, place.before)
    to_after = send(
        stream.at[frame_rows - HALO : frame_rows, :], halo.at[0], sems_h, 1, place.after
    )
    for p in inner:
        mix.third(p)
    for p in inner:
        place_stream(p)
    to_before.wait_recv()
    to_after.wait_recv()
    top = jnp.where(place.s == 0, 0.0, 1.0)
    bottom = jnp.where(place.s == seqs - 1, 0.0, 1.0)
    pad[0:HALO, :] = halo[0].astype(jnp.float32) * top
    pad[HALO + frame_rows : 2 * HALO + frame_rows, :] = halo[1].astype(jnp.float32) * bottom

    ring = Gather(place, whole, sems_g)
    order = (0, PIECES - 1) + tuple(range(1, PIECES - 1))

    def convolve(p):
        shift = HALO - KERNEL // 2
        total = jnp.zeros((rows, width), jnp.float32)
        for tap in range(KERNEL):
            total = total + taps_ref[tap : tap + 1, :] * pad[
                pl.ds(p * rows + tap + shift, rows), :
            ]
        at = slice(p * rows, (p + 1) * rows)
        value = pad[HALO + p * rows : HALO + (p + 1) * rows, :] + silu(total + bias_ref[...])
        value = value.astype(jnp.bfloat16)
        second[at, :] = value
        whole[at, own_cols] = value

    def feed(p):
        at = slice(p * rows, (p + 1) * rows)
        cells = whole[at, :].astype(jnp.float32)
        mean = jnp.mean(cells, axis=1, keepdims=True)
        centered = cells - mean
        var = jnp.mean(centered * centered, axis=1, keepdims=True)
        normed = (centered * lax.rsqrt(var + 1e-05) * gain_ref[...]).astype(jnp.bfloat16)
        upper = jnp.dot(normed, up[...], preferred_element_type=jnp.float32)
        hidden[at, :] = silu(upper).astype(jnp.bfloat16)

    for p in order:
        convolve(p)
        ring.first(p)
    for p in order:
        ring.second(p)
    for p in order[:2]:
        ring.third(p)
    get_up.wait()
    get_down.wait()
    ffn = Scatter(place, hidden, down, (relay_f, direct_f, sums_f, z_f, acc_f), sems_f)
    for i, p in enumerate(order):
        if i + 2 < PIECES:
            ring.third(order[i + 2])
        ring.last(p)
        feed(p)
        ffn.first(p)
        if i >= 1:
            ffn.second(order[i - 1])
        ffn.own(p)
        if i >= 2:
            ffn.third(order[i - 2])
    ffn.second(order[-1])
    for p in order[-2:]:
        ffn.third(p)
    for p in order:
        at = slice(p * rows, (p + 1) * rows)
        out_ref[at, :] = (second[at, :].astype(jnp.float32) + ffn.last(p)).astype(out_ref.dtype)
    for copy in back:
        copy.wait_send()
    mix.finish()
    to_before.wait_send()
    to_after.wait_send()
    ring.finish()
    ffn.finish()


def tail(attended, w_out, frames, taps, bias, gain, w_up, w_down):
    width = w_out.shape[0]
    frame_rows, depth = frames.shape
    hidden = w_up.shape[1]
    rows = frame_rows // PIECES
    vmem = pl.BlockSpec(memory_space=pltpu.VMEM)
    hbm = pl.BlockSpec(memory_space=pltpu.HBM)
    free = pl.BlockSpec(memory_space=pl.ANY)
    bf16, f32 = jnp.bfloat16, jnp.float32
    quarter = depth // 4
    buffers = [pltpu.VMEM((2, PIECES, rows, quarter), bf16)] * 3 + [
        pltpu.VMEM((2, PIECES, rows, width), bf16),
        pltpu.VMEM((PIECES, rows, quarter), f32),
    ]
    dma = pltpu.SemaphoreType.DMA
    return pl.pallas_call(
        functools.partial(tail_kernel, lax.axis_size("head"), lax.axis_size("seq")),
        in_specs=[free, hbm, hbm, vmem, vmem, vmem, hbm, hbm],
        out_specs=vmem,
        out_shape=jax.ShapeDtypeStruct((frame_rows, width), bf16),
        scratch_shapes=[
            pltpu.VMEM((width, depth), bf16),
            pltpu.VMEM((depth, hidden), bf16),
            pltpu.VMEM((hidden, depth), bf16),
            pltpu.VMEM((frame_rows, width), bf16),
            pltpu.VMEM((frame_rows, width), bf16),
            pltpu.VMEM((2, HALO, width), bf16),
            pltpu.VMEM((frame_rows + 2 * HALO, width), f32),
            pltpu.VMEM((frame_rows, width), bf16),
            pltpu.VMEM((frame_rows, depth), bf16),
            pltpu.VMEM((frame_rows, hidden), bf16),
        ]
        + buffers
        + buffers
        + [
            pltpu.VMEM((YS, frame_rows // 2, 2 * HD), bf16),
            pltpu.VMEM((frame_rows, width), bf16),
            dma((5,)),
            dma((2, YS)),
            dma((2, PIECES * 4)),
            dma((2, 2)),
            dma((2, PIECES * 6)),
            dma((2, PIECES * 4)),
        ],
        compiler_params=pltpu.CompilerParams(
            collective_id=0, has_side_effects=True, vmem_limit_bytes=44 * 1024 * 1024
        ),
        name="tail",
    )(attended, w_out, frames, taps, bias[None, :], gain[None, :], w_up, w_down)


def on_device(
    frames,
    w_query,
    w_key,
    w_value,
    w_out,
    conv_taps,
    conv_bias,
    norm_gain,
    w_up,
    w_down,
    block_lists,
    block_counts,
):
    kv_all, q_all, tables = front(
        frames, w_query, w_key, w_value, block_lists, block_counts
    )
    attended = attend_listed(tables, q_all, kv_all)
    return tail(attended, w_out, frames, conv_taps, conv_bias, norm_gain, w_up, w_down)


def solution(mesh):
    placed = (
        P("seq", None),
        P(None, "head"),
        P(None, "head"),
        P(None, "head"),
        P("head", None),
        P(None, "head"),
        P("head"),
        P(),
        P(None, "head"),
        P("head", None),
        P("seq", None),
        P("seq"),
    )
    return jax.shard_map(
        on_device, mesh=mesh, in_specs=placed, out_specs=P("seq", "head"), check_vma=False
    )
```

```python
import functools

import jax
import jax.numpy as jnp
from jax import lax
from jax.experimental import pallas as pl
from jax.experimental.pallas import tpu as pltpu
from jax.sharding import PartitionSpec as P

HD = 64
KERNEL = 31
NEG = -1e30


MESH = pl.DeviceIdType.MESH
PIECES = 4
HALO = 16
YS = 4
BLOCK = 128
SLOTS = 8
COUNT_ROW = 4
LIMIT = 66_322_432


def silu(v):
    return v / (1.0 + jnp.exp(-v))


class Place:
    def __init__(self, heads, seqs):
        self.me = lax.axis_index("head")
        ring = heads // 2
        self.x = lax.div(self.me, 2)
        self.z = lax.rem(self.me, 2)
        self.x_right = lax.rem(self.x + 1, ring)
        self.x_left = lax.rem(self.x + ring - 1, ring)
        self.x_far = lax.rem(self.x + 2, ring)
        self.right = {"head": self.x_right * 2 + self.z}
        self.left = {"head": self.x_left * 2 + self.z}
        self.partner = {"head": self.x * 2 + 1 - self.z}
        self.s = lax.axis_index("seq")
        self.core = lax.rem(self.s, 2)
        self.y = lax.rem(lax.div(self.s, 2), YS)
        self.zl = lax.div(self.s, 2 * YS)
        self.after = {"seq": lax.rem(self.s + 1, seqs)}
        self.before = {"seq": lax.rem(self.s + seqs - 1, seqs)}

    def greet(self):
        barrier = pltpu.get_barrier_semaphore()
        others = [self.right, self.left, self.partner, self.after, self.before]
        others += [self.far(d) for d in range(1, YS)]
        for other in others:
            pl.semaphore_signal(barrier, inc=1, device_id=other, device_id_type=MESH)
        pl.semaphore_wait(barrier, len(others))

    def seq_of(self, z_at, y_at, core_at):
        return (z_at * YS + y_at) * 2 + core_at

    def far(self, d):
        return {"seq": self.seq_of(self.zl, lax.rem(self.y + d, YS), self.core)}

    def ways(self, p):
        if p < PIECES // 2:
            return self.right, self.left, self.x_right, self.x_left
        return self.left, self.right, self.x_left, self.x_right


def send(src, dst, sems, key, device):
    copy = pltpu.make_async_remote_copy(
        src_ref=src,
        dst_ref=dst,
        send_sem=sems.at[0, key],
        recv_sem=sems.at[1, key],
        device_id=device,
        device_id_type=MESH,
    )
    copy.start()
    return copy


def swap(value):
    return pltpu.roll(value, HD, 1)


def front_kernel(
    frames_hbm,
    wq_hbm,
    wk_hbm,
    wv_hbm,
    w_out_hbm,
    lists_ref,
    counts_ref,
    kv_all,
    q_all,
    tables,
    w_mix,
    table,
    x,
    wq,
    wk,
    wv,
    kv_out,
    q_out,
    local_sems,
    sems,
    sems_w,
):
    frame_rows = x.shape[0]
    half = frame_rows // 2
    f32, bf16 = jnp.float32, jnp.bfloat16
    loads = []
    for i, (src, dst) in enumerate(
        ((frames_hbm, x), (wk_hbm, wk), (wv_hbm, wv), (wq_hbm, wq))
    ):
        load = pltpu.make_async_copy(src, dst, local_sems.at[i])
        load.start()
        loads.append(load)

    table[...] = jnp.zeros_like(table)
    table[: lists_ref.shape[0], : lists_ref.shape[1]] = lists_ref[...]
    table[COUNT_ROW : COUNT_ROW + 1, : counts_ref.shape[1]] = counts_ref[...]

    s = lax.axis_index("seq")
    core = lax.rem(s, 2)
    y = lax.rem(lax.div(s, 2), YS)
    zl = lax.div(s, 2 * YS)

    def seq_of(z_at, y_at, core_at):
        return (z_at * YS + y_at) * 2 + core_at

    def far(d):
        return {"seq": seq_of(zl, lax.rem(y + d, YS), core)}

    mate = {"seq": seq_of(zl, y, 1 - core)}
    across = {"seq": seq_of(1 - zl, y, core)}
    barrier = pltpu.get_barrier_semaphore()
    head = lax.axis_index("head")
    heads = w_mix.shape[0] // w_mix.shape[1]

    def head_at(d):
        return lax.rem(head + d, heads)

    others = [far(d) for d in range(1, YS)] + [mate, across]
    others += [{"head": head_at(d)} for d in range(1, heads)]
    for other in others:
        pl.semaphore_signal(barrier, inc=1, device_id=other, device_id_type=MESH)
    pl.semaphore_wait(barrier, len(others))

    width = w_mix.shape[1]
    share = width // 2

    def mix_rows(t):
        start = pl.multiple_of(t * width + core * share, share)
        return w_mix.at[pl.ds(start, share), :]

    def w_cols(t):
        return pl.ds(pl.multiple_of(t * width, width), width)

    sent = {}
    for d in (3, 5, 4, 1, 7, 2, 6):
        mine = w_out_hbm.at[pl.ds(pl.multiple_of(core * share, share), share), w_cols(head_at(d))]
        sent["w", d] = send(mine, mix_rows(head), sems_w, d, {"head": head_at(d)})
    own_mix = pltpu.make_async_copy(
        w_out_hbm.at[:, w_cols(head)], w_mix.at[w_cols(head), :], local_sems.at[7]
    )
    own_mix.start()

    low = lax.broadcasted_iota(jnp.int32, (half, 2 * HD), 1) < HD
    for load in loads[:3]:
        load.wait()
    for part in range(2):
        rows = slice(part * half, (part + 1) * half)
        k = jnp.dot(x[rows, :], wk[...], preferred_element_type=f32)
        v = jnp.dot(x[rows, :], wv[...], preferred_element_type=f32)
        for pair in range(YS // 2):
            cols = slice(pair * 2 * HD, (pair + 1) * 2 * HD)
            kp, vp = k[:, cols], v[:, cols]
            kv_out[2 * pair, rows, :] = jnp.where(low, kp, swap(vp)).astype(bf16)
            kv_out[2 * pair + 1, rows, :] = jnp.where(low, swap(kp), vp).astype(bf16)

    def rows_of(z_at, y_at, core_at):
        start = seq_of(z_at, y_at, core_at) * frame_rows
        return kv_all.at[pl.ds(pl.multiple_of(start, frame_rows), frame_rows), :]

    here = rows_of(zl, y, core)
    for d in (2, 1, 3):
        to = lax.rem(y + d, YS)
        sent["kv", d] = send(kv_out.at[to], here, sems, d, far(d))
        sent["table", d] = send(table, tables.at[y], sems, 4 + d, far(d))
    sent["across", 0] = send(kv_out.at[y], here, sems, 8, across)
    sent["mate", 0] = send(kv_out.at[y], here, sems, 12, mate)
    keep = [
        pltpu.make_async_copy(kv_out.at[y], here, local_sems.at[4]),
        pltpu.make_async_copy(table, tables.at[y], local_sems.at[5]),
    ]
    for copy in keep:
        copy.start()

    loads[3].wait()
    q = 0.125 * jnp.dot(x[...], wq[...], preferred_element_type=f32)
    for pair in range(YS // 2):
        cols = slice(pair * 2 * HD, (pair + 1) * 2 * HD)
        top, bottom = q[:half, cols], q[half:, cols]
        q_out[2 * pair] = jnp.where(low, top, swap(bottom)).astype(bf16)
        q_out[2 * pair + 1] = jnp.where(low, swap(top), bottom).astype(bf16)
    for d in (2, 1, 3):
        to = lax.rem(y + d, YS)
        sent["q", d] = send(q_out.at[to], q_all.at[y], sems, 20 + d, far(d))
    keep.append(pltpu.make_async_copy(q_out.at[y], q_all.at[y], local_sems.at[6]))
    keep[-1].start()

    for d in (1, 3, 2):
        sent["kv", d].wait_recv()
        piece = rows_of(zl, lax.rem(y + YS - d, YS), core)
        sent["across", d] = send(piece, piece, sems, 8 + d, across)
        sent["mate", d] = send(piece, piece, sems, 12 + d, mate)
    for d in (0, 1, 3, 2):
        sent["across", d].wait_recv()
        piece = rows_of(1 - zl, lax.rem(y + YS - d, YS), core)
        sent["over", d] = send(piece, piece, sems, 16 + d, mate)
    for d in range(1, heads):
        sent["w", d].wait_recv()
        piece = mix_rows(head_at(heads - d))
        sent["w_mate", d] = send(piece, piece, sems_w, heads + d, mate)
    for d in range(1, YS):
        sent["table", d].wait_recv()
    for d in range(1, YS):
        sent["q", d].wait_recv()
    for d in range(YS):
        sent["mate", d].wait_recv()
    for d in range(YS):
        sent["over", d].wait_recv()
    for d in range(1, heads):
        sent["w_mate", d].wait_recv()
    own_mix.wait()
    for copy in keep:
        copy.wait()
    for copy in sent.values():
        copy.wait_send()


def attention_kernel(tables_ref, q_ref, kv_ref, out_ref):
    f32, bf16 = jnp.float32, jnp.bfloat16
    sources, half, lanes = q_ref.shape
    block, slots = BLOCK, SLOTS
    per_half = half // block
    low = lax.broadcasted_iota(jnp.int32, (block, lanes), 1) < HD
    slot_col = lax.broadcasted_iota(jnp.int32, (block, slots * block), 1)

    def attend(source, b):
        packed = q_ref[source, (b % per_half) * block : (b % per_half + 1) * block, :]
        packed = packed.astype(f32)
        if b >= per_half:
            packed = swap(packed)
        query = jnp.where(low, packed, 0.0).astype(bf16)
        cells = []
        for j in range(slots):
            start = pl.multiple_of(tables_ref[source, b, j] * block, block)
            cells.append(kv_ref[pl.ds(start, block), :])
        kv = jnp.concatenate(cells, axis=0)
        scores = lax.dot_general(query, kv, (((1,), (1,)), ((), ())), preferred_element_type=f32)
        live = slot_col < tables_ref[source, COUNT_ROW, b] * block
        scores = jnp.where(live, scores, NEG)
        top = jnp.max(scores, axis=1, keepdims=True)
        p = jnp.exp(scores - top)
        total = jnp.sum(p, axis=1, keepdims=True)
        return jnp.dot(p.astype(bf16), kv, preferred_element_type=f32) / total

    for source in range(sources):
        for b in range(per_half):
            early, late = attend(source, b), attend(source, b + per_half)
            rows = slice(b * block, (b + 1) * block)
            out_ref[source, rows, :] = jnp.where(low, swap(early), late).astype(bf16)


def attend_listed(tables, q_all, kv_all):
    vmem = pl.BlockSpec(memory_space=pltpu.VMEM)
    return pl.pallas_call(
        attention_kernel,
        in_specs=[pl.BlockSpec(memory_space=pltpu.SMEM), vmem, vmem],
        out_specs=vmem,
        out_shape=jax.ShapeDtypeStruct(q_all.shape, jnp.bfloat16),
        compiler_params=pltpu.CompilerParams(vmem_limit_bytes=LIMIT),
        name="attend",
    )(tables, q_all, kv_all)


def front(frames, w_query, w_key, w_value, w_out, lists, counts):
    frame_rows, depth = frames.shape
    width = w_query.shape[1]
    seqs = lax.axis_size("seq")
    bf16 = jnp.bfloat16
    hbm = pl.BlockSpec(memory_space=pltpu.HBM)
    free = pl.BlockSpec(memory_space=pl.ANY)
    vmem = pl.BlockSpec(memory_space=pltpu.VMEM)
    dma = pltpu.SemaphoreType.DMA
    lanes = 2 * HD
    return pl.pallas_call(
        front_kernel,
        in_specs=[hbm, hbm, hbm, hbm, hbm, vmem, vmem],
        out_specs=[free, free, free, free],
        out_shape=[
            jax.ShapeDtypeStruct((seqs * frame_rows, lanes), bf16),
            jax.ShapeDtypeStruct((YS, frame_rows // 2, lanes), bf16),
            jax.ShapeDtypeStruct((YS, 8, 128), jnp.int32),
            jax.ShapeDtypeStruct((depth, width), bf16),
        ],
        scratch_shapes=[
            pltpu.VMEM((8, 128), jnp.int32),
            pltpu.VMEM((frame_rows, depth), bf16),
            pltpu.VMEM((depth, width), bf16),
            pltpu.VMEM((depth, width), bf16),
            pltpu.VMEM((depth, width), bf16),
            pltpu.VMEM((YS, frame_rows, lanes), bf16),
            pltpu.VMEM((YS, frame_rows // 2, lanes), bf16),
            dma((8,)),
            dma((2, 24)),
            dma((2, 16)),
        ],
        compiler_params=pltpu.CompilerParams(
            collective_id=1, has_side_effects=True, vmem_limit_bytes=LIMIT
        ),
        name="front",
    )(frames, w_query, w_key, w_value, w_out, lists, counts[None, :])


class Scatter:
    def __init__(self, place, a, w, bufs, sems):
        self.place, self.a, self.w = place, a, w
        (self.relay, self.direct, self.sums, self.zbuf, self.acc) = bufs
        self.sems = sems
        self.rows = a.shape[0] // PIECES
        self.width = w.shape[1] // 4
        self.copies = {}

    def part(self, p, xd):
        cols = pl.ds(pl.multiple_of(xd * self.width, self.width), self.width)
        return jnp.dot(
            self.a[p * self.rows : (p + 1) * self.rows, :],
            self.w[:, cols],
            preferred_element_type=jnp.float32,
        )

    def go(self, p, kind, buf, device):
        self.copies[p, kind] = send(
            buf.at[0, p], buf.at[1, p], self.sems, p * 4 + kind, device
        )

    def first(self, p):
        fwd, bwd, x_fwd, x_bwd = self.place.ways(p)
        self.relay[0, p] = self.part(p, self.place.x_far).astype(jnp.bfloat16)
        self.go(p, 0, self.relay, fwd)
        self.direct[0, p] = self.part(p, x_bwd).astype(jnp.bfloat16)
        self.go(p, 1, self.direct, bwd)

    def second(self, p):
        fwd, bwd, x_fwd, x_bwd = self.place.ways(p)
        mine = self.part(p, x_fwd)
        self.copies[p, 0].wait_recv()
        self.sums[0, p] = (mine + self.relay[1, p].astype(jnp.float32)).astype(jnp.bfloat16)
        self.go(p, 2, self.sums, fwd)

    def own(self, p):
        self.acc[p] = self.part(p, self.place.x)

    def third(self, p):
        self.copies[p, 1].wait_recv()
        self.copies[p, 2].wait_recv()
        self.acc[p] = (
            self.acc[p]
            + self.direct[1, p].astype(jnp.float32)
            + self.sums[1, p].astype(jnp.float32)
        )
        half = self.width // 2
        other = pl.ds(pl.multiple_of((1 - self.place.z) * half, half), half)
        self.zbuf[0, p] = self.acc[p, :, other].astype(jnp.bfloat16)
        self.go(p, 3, self.zbuf, self.place.partner)

    def last(self, p):
        self.copies[p, 3].wait_recv()
        half = self.width // 2
        kept = pl.ds(pl.multiple_of(self.place.z * half, half), half)
        return self.acc[p, :, kept] + self.zbuf[1, p].astype(jnp.float32)

    def finish(self):
        for copy in self.copies.values():
            copy.wait_send()


class Gather:
    def __init__(self, place, whole, sems):
        self.place, self.whole, self.sems = place, whole, sems
        self.rows = whole.shape[0] // PIECES
        self.width = whole.shape[1] // 8
        self.copies = {}

    def view(self, p, head, count):
        width = self.width
        cols = pl.ds(pl.multiple_of(head * width, width), count * width)
        return self.whole.at[p * self.rows : (p + 1) * self.rows, cols]

    def go(self, p, kind, head, count, device):
        view = self.view(p, head, count)
        self.copies[p, kind] = send(view, view, self.sems, p * 6 + kind, device)

    def first(self, p):
        fwd, bwd, x_fwd, x_bwd = self.place.ways(p)
        self.go(p, 0, self.place.me, 1, self.place.partner)
        self.go(p, 1, self.place.me, 1, fwd)
        self.go(p, 2, self.place.me, 1, bwd)

    def second(self, p):
        fwd, bwd, x_fwd, x_bwd = self.place.ways(p)
        self.copies[p, 0].wait_recv()
        mate = self.place.x * 2 + 1 - self.place.z
        self.go(p, 3, mate, 1, fwd)
        self.go(p, 4, mate, 1, bwd)

    def third(self, p):
        fwd, bwd, x_fwd, x_bwd = self.place.ways(p)
        self.copies[p, 1].wait_recv()
        self.copies[p, 3].wait_recv()
        self.go(p, 5, x_bwd * 2, 2, fwd)

    def last(self, p):
        self.copies[p, 2].wait_recv()
        self.copies[p, 4].wait_recv()
        self.copies[p, 5].wait_recv()

    def finish(self):
        for copy in self.copies.values():
            copy.wait_send()


def tail_kernel(
    heads,
    seqs,
    att_ref,
    w_mix_hbm,
    frames_hbm,
    taps_ref,
    bias_ref,
    gain_ref,
    up_hbm,
    down_hbm,
    out_ref,
    w_mix,
    up,
    down,
    resid,
    stream,
    halo,
    pad,
    second,
    whole,
    hidden,
    relay_f,
    direct_f,
    sums_f,
    z_f,
    acc_f,
    ret_in,
    joined,
    local_sems,
    sems_r,
    sems_o,
    sems_h,
    sems_g,
    sems_f,
):
    place = Place(heads, seqs)
    frame_rows, width = out_ref.shape
    rows = frame_rows // PIECES
    own_cols = pl.ds(pl.multiple_of(place.me * width, width), width)
    get_resid = pltpu.make_async_copy(frames_hbm.at[:, own_cols], resid, local_sems.at[0])
    get_up = pltpu.make_async_copy(up_hbm, up, local_sems.at[1])
    get_down = pltpu.make_async_copy(down_hbm, down, local_sems.at[2])
    get_mix = pltpu.make_async_copy(w_mix_hbm, w_mix, local_sems.at[4])
    get_mix.start()
    get_resid.start()
    get_up.start()
    get_down.start()
    place.greet()

    back = [
        send(att_ref.at[lax.rem(place.y + d, YS)], ret_in.at[place.y], sems_r, d, place.far(d))
        for d in (2, 1, 3)
    ]
    own_back = pltpu.make_async_copy(
        att_ref.at[place.y], ret_in.at[place.y], local_sems.at[3]
    )
    own_back.start()
    half = frame_rows // 2
    low = lax.broadcasted_iota(jnp.int32, (half, 2 * HD), 1) < HD
    own_back.wait()
    for copy in back:
        copy.wait_recv()
    for pair in range(YS // 2):
        cols = pl.ds(pl.multiple_of(place.me * width + pair * 2 * HD, 2 * HD), 2 * HD)
        one, two = ret_in[2 * pair].astype(jnp.float32), ret_in[2 * pair + 1].astype(jnp.float32)
        joined[:half, cols] = jnp.where(low, one, swap(two)).astype(jnp.bfloat16)
        joined[half:, cols] = jnp.where(low, swap(one), two).astype(jnp.bfloat16)

    order = (0, PIECES - 1) + tuple(range(1, PIECES - 1))
    mix = Gather(place, joined, sems_o)
    for p in order:
        mix.first(p)
    for p in order:
        mix.second(p)
    for p in order:
        mix.third(p)
    get_resid.wait()
    get_mix.wait()

    def place_stream(p):
        at = slice(p * rows, (p + 1) * rows)
        mix.last(p)
        mixed = jnp.dot(joined[at, :], w_mix[...], preferred_element_type=jnp.float32)
        value = (resid[at, :].astype(jnp.float32) + mixed).astype(jnp.bfloat16)
        stream[at, :] = value
        pad[HALO + p * rows : HALO + (p + 1) * rows, :] = value.astype(jnp.float32)

    for p in order[:2]:
        place_stream(p)
    to_before = send(stream.at[0:HALO, :], halo.at[1], sems_h, 0, place.before)
    to_after = send(
        stream.at[frame_rows - HALO : frame_rows, :], halo.at[0], sems_h, 1, place.after
    )
    for p in order[2:]:
        place_stream(p)
    to_before.wait_recv()
    to_after.wait_recv()
    top = jnp.where(place.s == 0, 0.0, 1.0)
    bottom = jnp.where(place.s == seqs - 1, 0.0, 1.0)
    pad[0:HALO, :] = halo[0].astype(jnp.float32) * top
    pad[HALO + frame_rows : 2 * HALO + frame_rows, :] = halo[1].astype(jnp.float32) * bottom

    ring = Gather(place, whole, sems_g)

    def convolve(p):
        shift = HALO - KERNEL // 2
        total = jnp.zeros((rows, width), jnp.float32)
        for tap in range(KERNEL):
            total = total + taps_ref[tap : tap + 1, :] * pad[
                pl.ds(p * rows + tap + shift, rows), :
            ]
        at = slice(p * rows, (p + 1) * rows)
        value = pad[HALO + p * rows : HALO + (p + 1) * rows, :] + silu(total + bias_ref[...])
        value = value.astype(jnp.bfloat16)
        second[at, :] = value
        whole[at, own_cols] = value

    def feed(p):
        at = slice(p * rows, (p + 1) * rows)
        cells = whole[at, :].astype(jnp.float32)
        mean = jnp.mean(cells, axis=1, keepdims=True)
        centered = cells - mean
        var = jnp.mean(centered * centered, axis=1, keepdims=True)
        normed = (centered * lax.rsqrt(var + 1e-05) * gain_ref[...]).astype(jnp.bfloat16)
        upper = jnp.dot(normed, up[...], preferred_element_type=jnp.float32)
        hidden[at, :] = silu(upper).astype(jnp.bfloat16)

    for p in order:
        convolve(p)
        ring.first(p)
    for p in order:
        ring.second(p)
    for p in order[:2]:
        ring.third(p)
    get_up.wait()
    get_down.wait()
    ffn = Scatter(place, hidden, down, (relay_f, direct_f, sums_f, z_f, acc_f), sems_f)
    for i, p in enumerate(order):
        if i + 2 < PIECES:
            ring.third(order[i + 2])
        ring.last(p)
        feed(p)
        ffn.first(p)
        if i >= 1:
            ffn.second(order[i - 1])
        ffn.own(p)
        if i >= 2:
            ffn.third(order[i - 2])
    ffn.second(order[-1])
    for p in order[-2:]:
        ffn.third(p)
    for p in order:
        at = slice(p * rows, (p + 1) * rows)
        out_ref[at, :] = (second[at, :].astype(jnp.float32) + ffn.last(p)).astype(out_ref.dtype)
    for copy in back:
        copy.wait_send()
    mix.finish()
    to_before.wait_send()
    to_after.wait_send()
    ring.finish()
    ffn.finish()


def tail(attended, w_mix, frames, taps, bias, gain, w_up, w_down):
    width = w_mix.shape[1]
    frame_rows, depth = frames.shape
    hidden = w_up.shape[1]
    rows = frame_rows // PIECES
    vmem = pl.BlockSpec(memory_space=pltpu.VMEM)
    hbm = pl.BlockSpec(memory_space=pltpu.HBM)
    free = pl.BlockSpec(memory_space=pl.ANY)
    bf16, f32 = jnp.bfloat16, jnp.float32
    quarter = depth // 4
    buffers = [pltpu.VMEM((2, PIECES, rows, quarter), bf16)] * 3 + [
        pltpu.VMEM((2, PIECES, rows, width), bf16),
        pltpu.VMEM((PIECES, rows, quarter), f32),
    ]
    dma = pltpu.SemaphoreType.DMA
    return pl.pallas_call(
        functools.partial(tail_kernel, lax.axis_size("head"), lax.axis_size("seq")),
        in_specs=[free, hbm, hbm, vmem, vmem, vmem, hbm, hbm],
        out_specs=vmem,
        out_shape=jax.ShapeDtypeStruct((frame_rows, width), bf16),
        scratch_shapes=[
            pltpu.VMEM((depth, width), bf16),
            pltpu.VMEM((depth, hidden), bf16),
            pltpu.VMEM((hidden, depth), bf16),
            pltpu.VMEM((frame_rows, width), bf16),
            pltpu.VMEM((frame_rows, width), bf16),
            pltpu.VMEM((2, HALO, width), bf16),
            pltpu.VMEM((frame_rows + 2 * HALO, width), f32),
            pltpu.VMEM((frame_rows, width), bf16),
            pltpu.VMEM((frame_rows, depth), bf16),
            pltpu.VMEM((frame_rows, hidden), bf16),
        ]
        + buffers
        + [
            pltpu.VMEM((YS, frame_rows // 2, 2 * HD), bf16),
            pltpu.VMEM((frame_rows, depth), bf16),
            dma((5,)),
            dma((2, YS)),
            dma((2, PIECES * 6)),
            dma((2, 2)),
            dma((2, PIECES * 6)),
            dma((2, PIECES * 4)),
        ],
        compiler_params=pltpu.CompilerParams(
            collective_id=0, has_side_effects=True, vmem_limit_bytes=LIMIT
        ),
        name="tail",
    )(attended, w_mix, frames, taps, bias[None, :], gain[None, :], w_up, w_down)


def on_device(
    frames,
    w_query,
    w_key,
    w_value,
    w_out,
    conv_taps,
    conv_bias,
    norm_gain,
    w_up,
    w_down,
    block_lists,
    block_counts,
):
    kv_all, q_all, tables, w_mix = front(
        frames, w_query, w_key, w_value, w_out, block_lists, block_counts
    )
    attended = attend_listed(tables, q_all, kv_all)
    return tail(attended, w_mix, frames, conv_taps, conv_bias, norm_gain, w_up, w_down)


def solution(mesh):
    placed = (
        P("seq", None),
        P(None, "head"),
        P(None, "head"),
        P(None, "head"),
        P("head", None),
        P(None, "head"),
        P("head"),
        P(),
        P(None, "head"),
        P("head", None),
        P("seq", None),
        P("seq"),
    )
    return jax.shard_map(
        on_device, mesh=mesh, in_specs=placed, out_specs=P("seq", "head"), check_vma=False
    )
```

```python
import functools

import jax
import jax.numpy as jnp
from jax import lax
from jax.experimental import pallas as pl
from jax.experimental.pallas import tpu as pltpu
from jax.sharding import PartitionSpec as P

HD = 64
KERNEL = 31
NEG = -1e30


MESH = pl.DeviceIdType.MESH
PIECES = 4
LAG = PIECES // 4
ORDER = (0, 2, 1, 3)
INSIDE, EDGES = (1, 2), (0, 3)
HALO = 16
YS = 4
BLOCK = 128
SLOTS = 8
COUNT_ROW = 4
FRONT_LIMIT = 66322432
LIMIT = 66322432


def silu(v):
    return v / (1.0 + jnp.exp(-v))


class Place:
    def __init__(self, heads, seqs):
        self.me = lax.axis_index("head")
        ring = heads // 2
        self.x = lax.div(self.me, 2)
        self.z = lax.rem(self.me, 2)
        self.x_right = lax.rem(self.x + 1, ring)
        self.x_left = lax.rem(self.x + ring - 1, ring)
        self.x_far = lax.rem(self.x + 2, ring)
        self.right = {"head": self.x_right * 2 + self.z}
        self.left = {"head": self.x_left * 2 + self.z}
        self.partner = {"head": self.x * 2 + 1 - self.z}
        self.s = lax.axis_index("seq")
        self.core = lax.rem(self.s, 2)
        self.y = lax.rem(lax.div(self.s, 2), YS)
        self.zl = lax.div(self.s, 2 * YS)
        self.after = {"seq": lax.rem(self.s + 1, seqs)}
        self.before = {"seq": lax.rem(self.s + seqs - 1, seqs)}

    def greet(self):
        barrier = pltpu.get_barrier_semaphore()
        others = [self.right, self.left, self.partner, self.after, self.before]
        others += [self.far(d) for d in range(1, YS)]
        for other in others:
            pl.semaphore_signal(barrier, inc=1, device_id=other, device_id_type=MESH)
        pl.semaphore_wait(barrier, len(others))

    def seq_of(self, z_at, y_at, core_at):
        return (z_at * YS + y_at) * 2 + core_at

    def far(self, d):
        return {"seq": self.seq_of(self.zl, lax.rem(self.y + d, YS), self.core)}

    def ways(self, p):
        if p < PIECES // 2:
            return self.right, self.left, self.x_right, self.x_left
        return self.left, self.right, self.x_left, self.x_right


def send(src, dst, sems, key, device):
    copy = pltpu.make_async_remote_copy(
        src_ref=src,
        dst_ref=dst,
        send_sem=sems.at[0, key],
        recv_sem=sems.at[1, key],
        device_id=device,
        device_id_type=MESH,
    )
    copy.start()
    return copy


def swap(value):
    return pltpu.roll(value, HD, 1)


def front_kernel(
    frames_hbm,
    wq_hbm,
    wk_hbm,
    wv_hbm,
    w_out_hbm,
    lists_ref,
    counts_ref,
    kv_all,
    q_all,
    tables,
    w_mix,
    table,
    x,
    wq,
    wk,
    wv,
    kv_out,
    q_out,
    local_sems,
    sems,
    sems_w,
):
    frame_rows = x.shape[0]
    half = frame_rows // 2
    f32, bf16 = jnp.float32, jnp.bfloat16
    loads = []
    for i, (src, dst) in enumerate(
        ((frames_hbm, x), (wk_hbm, wk), (wv_hbm, wv), (wq_hbm, wq))
    ):
        load = pltpu.make_async_copy(src, dst, local_sems.at[i])
        load.start()
        loads.append(load)

    table[...] = jnp.zeros_like(table)
    table[: lists_ref.shape[0], : lists_ref.shape[1]] = lists_ref[...]
    table[COUNT_ROW : COUNT_ROW + 1, : counts_ref.shape[1]] = counts_ref[...]

    s = lax.axis_index("seq")
    core = lax.rem(s, 2)
    y = lax.rem(lax.div(s, 2), YS)
    zl = lax.div(s, 2 * YS)

    def seq_of(z_at, y_at, core_at):
        return (z_at * YS + y_at) * 2 + core_at

    def far(d):
        return {"seq": seq_of(zl, lax.rem(y + d, YS), core)}

    mate = {"seq": seq_of(zl, y, 1 - core)}
    across = {"seq": seq_of(1 - zl, y, core)}
    barrier = pltpu.get_barrier_semaphore()
    head = lax.axis_index("head")
    heads = w_mix.shape[0] // w_mix.shape[1]

    def head_at(d):
        return lax.rem(head + d, heads)

    others = [far(d) for d in range(1, YS)] + [mate, across]
    others += [{"head": head_at(d)} for d in range(1, heads)]
    for other in others:
        pl.semaphore_signal(barrier, inc=1, device_id=other, device_id_type=MESH)
    pl.semaphore_wait(barrier, len(others))

    width = w_mix.shape[1]
    share = width // 2

    def mix_rows(t):
        start = pl.multiple_of(t * width + core * share, share)
        return w_mix.at[pl.ds(start, share), :]

    def w_cols(t):
        return pl.ds(pl.multiple_of(t * width, width), width)

    sent = {}
    for d in (3, 5, 4, 1, 7, 2, 6):
        mine = w_out_hbm.at[pl.ds(pl.multiple_of(core * share, share), share), w_cols(head_at(d))]
        sent["w", d] = send(mine, mix_rows(head), sems_w, d, {"head": head_at(d)})
    own_mix = pltpu.make_async_copy(
        w_out_hbm.at[:, w_cols(head)], w_mix.at[w_cols(head), :], local_sems.at[7]
    )
    own_mix.start()

    low = lax.broadcasted_iota(jnp.int32, (half, 2 * HD), 1) < HD
    for load in loads[:3]:
        load.wait()
    for part in range(2):
        rows = slice(part * half, (part + 1) * half)
        k = jnp.dot(x[rows, :], wk[...], preferred_element_type=f32)
        v = jnp.dot(x[rows, :], wv[...], preferred_element_type=f32)
        for pair in range(YS // 2):
            cols = slice(pair * 2 * HD, (pair + 1) * 2 * HD)
            kp, vp = k[:, cols], v[:, cols]
            kv_out[2 * pair, rows, :] = jnp.where(low, kp, swap(vp)).astype(bf16)
            kv_out[2 * pair + 1, rows, :] = jnp.where(low, swap(kp), vp).astype(bf16)

    def rows_of(z_at, y_at, core_at):
        start = seq_of(z_at, y_at, core_at) * frame_rows
        return kv_all.at[pl.ds(pl.multiple_of(start, frame_rows), frame_rows), :]

    here = rows_of(zl, y, core)
    for d in (2, 1, 3):
        to = lax.rem(y + d, YS)
        sent["kv", d] = send(kv_out.at[to], here, sems, d, far(d))
        sent["table", d] = send(table, tables.at[y], sems, 4 + d, far(d))
    sent["across", 0] = send(kv_out.at[y], here, sems, 8, across)
    sent["mate", 0] = send(kv_out.at[y], here, sems, 12, mate)
    keep = [
        pltpu.make_async_copy(kv_out.at[y], here, local_sems.at[4]),
        pltpu.make_async_copy(table, tables.at[y], local_sems.at[5]),
    ]
    for copy in keep:
        copy.start()

    loads[3].wait()
    q = 0.125 * jnp.dot(x[...], wq[...], preferred_element_type=f32)
    for pair in range(YS // 2):
        cols = slice(pair * 2 * HD, (pair + 1) * 2 * HD)
        top, bottom = q[:half, cols], q[half:, cols]
        q_out[2 * pair] = jnp.where(low, top, swap(bottom)).astype(bf16)
        q_out[2 * pair + 1] = jnp.where(low, swap(top), bottom).astype(bf16)
    for d in (2, 1, 3):
        to = lax.rem(y + d, YS)
        sent["q", d] = send(q_out.at[to], q_all.at[y], sems, 20 + d, far(d))
    keep.append(pltpu.make_async_copy(q_out.at[y], q_all.at[y], local_sems.at[6]))
    keep[-1].start()

    for d in (1, 3, 2):
        sent["kv", d].wait_recv()
        piece = rows_of(zl, lax.rem(y + YS - d, YS), core)
        sent["across", d] = send(piece, piece, sems, 8 + d, across)
        sent["mate", d] = send(piece, piece, sems, 12 + d, mate)
    for d in (0, 1, 3, 2):
        sent["across", d].wait_recv()
        piece = rows_of(1 - zl, lax.rem(y + YS - d, YS), core)
        sent["over", d] = send(piece, piece, sems, 16 + d, mate)
    for d in range(1, heads):
        sent["w", d].wait_recv()
        piece = mix_rows(head_at(heads - d))
        sent["w_mate", d] = send(piece, piece, sems_w, heads + d, mate)
    for d in range(1, YS):
        sent["table", d].wait_recv()
    for d in range(1, YS):
        sent["q", d].wait_recv()
    for d in range(YS):
        sent["mate", d].wait_recv()
    for d in range(YS):
        sent["over", d].wait_recv()
    for d in range(1, heads):
        sent["w_mate", d].wait_recv()
    own_mix.wait()
    for copy in keep:
        copy.wait()
    for copy in sent.values():
        copy.wait_send()


def attention_kernel(tables_ref, q_ref, kv_ref, out_ref):
    f32, bf16 = jnp.float32, jnp.bfloat16
    sources, half, lanes = q_ref.shape
    block, slots = BLOCK, SLOTS
    per_half = half // block
    low = lax.broadcasted_iota(jnp.int32, (block, lanes), 1) < HD
    slot_col = lax.broadcasted_iota(jnp.int32, (block, slots * block), 1)

    def attend(source, b):
        packed = q_ref[source, (b % per_half) * block : (b % per_half + 1) * block, :]
        packed = packed.astype(f32)
        if b >= per_half:
            packed = swap(packed)
        query = jnp.where(low, packed, 0.0).astype(bf16)
        cells = []
        for j in range(slots):
            start = pl.multiple_of(tables_ref[source, b, j] * block, block)
            cells.append(kv_ref[pl.ds(start, block), :])
        kv = jnp.concatenate(cells, axis=0)
        scores = lax.dot_general(query, kv, (((1,), (1,)), ((), ())), preferred_element_type=f32)
        live = slot_col < tables_ref[source, COUNT_ROW, b] * block
        scores = jnp.where(live, scores, NEG)
        top = jnp.max(scores, axis=1, keepdims=True)
        p = jnp.exp(scores - top)
        total = jnp.sum(p, axis=1, keepdims=True)
        return jnp.dot(p.astype(bf16), kv, preferred_element_type=f32) / total

    for source in range(sources):
        for b in range(per_half):
            early, late = attend(source, b), attend(source, b + per_half)
            rows = slice(b * block, (b + 1) * block)
            out_ref[source, rows, :] = jnp.where(low, swap(early), late).astype(bf16)


def attend_listed(tables, q_all, kv_all):
    vmem = pl.BlockSpec(memory_space=pltpu.VMEM)
    return pl.pallas_call(
        attention_kernel,
        in_specs=[pl.BlockSpec(memory_space=pltpu.SMEM), vmem, vmem],
        out_specs=vmem,
        out_shape=jax.ShapeDtypeStruct(q_all.shape, jnp.bfloat16),
        compiler_params=pltpu.CompilerParams(vmem_limit_bytes=LIMIT),
        name="attend",
    )(tables, q_all, kv_all)


def front(frames, w_query, w_key, w_value, w_out, lists, counts):
    frame_rows, depth = frames.shape
    width = w_query.shape[1]
    seqs = lax.axis_size("seq")
    bf16 = jnp.bfloat16
    hbm = pl.BlockSpec(memory_space=pltpu.HBM)
    free = pl.BlockSpec(memory_space=pl.ANY)
    vmem = pl.BlockSpec(memory_space=pltpu.VMEM)
    dma = pltpu.SemaphoreType.DMA
    lanes = 2 * HD
    return pl.pallas_call(
        front_kernel,
        in_specs=[hbm, hbm, hbm, hbm, hbm, vmem, vmem],
        out_specs=[free, free, free, free],
        out_shape=[
            jax.ShapeDtypeStruct((seqs * frame_rows, lanes), bf16),
            jax.ShapeDtypeStruct((YS, frame_rows // 2, lanes), bf16),
            jax.ShapeDtypeStruct((YS, 8, 128), jnp.int32),
            jax.ShapeDtypeStruct((depth, width), bf16),
        ],
        scratch_shapes=[
            pltpu.VMEM((8, 128), jnp.int32),
            pltpu.VMEM((frame_rows, depth), bf16),
            pltpu.VMEM((depth, width), bf16),
            pltpu.VMEM((depth, width), bf16),
            pltpu.VMEM((depth, width), bf16),
            pltpu.VMEM((YS, frame_rows, lanes), bf16),
            pltpu.VMEM((YS, frame_rows // 2, lanes), bf16),
            dma((8,)),
            dma((2, 24)),
            dma((2, 16)),
        ],
        compiler_params=pltpu.CompilerParams(
            collective_id=1, has_side_effects=True, vmem_limit_bytes=FRONT_LIMIT
        ),
        name="front",
    )(frames, w_query, w_key, w_value, w_out, lists, counts[None, :])


class Scatter:
    def __init__(self, place, a, w, bufs, sems):
        self.place, self.a, self.w = place, a, w
        (self.relay, self.direct, self.sums, self.zbuf, self.acc) = bufs
        self.sems = sems
        self.rows = a.shape[0] // PIECES
        self.width = w.shape[1] // 4
        self.copies = {}

    def part(self, p, xd):
        cols = pl.ds(pl.multiple_of(xd * self.width, self.width), self.width)
        return jnp.dot(
            self.a[p * self.rows : (p + 1) * self.rows, :],
            self.w[:, cols],
            preferred_element_type=jnp.float32,
        )

    def go(self, p, kind, buf, device):
        self.copies[p, kind] = send(
            buf.at[0, p], buf.at[1, p], self.sems, p * 4 + kind, device
        )

    def first(self, p):
        fwd, bwd, x_fwd, x_bwd = self.place.ways(p)
        self.relay[0, p] = self.part(p, self.place.x_far).astype(jnp.bfloat16)
        self.go(p, 0, self.relay, fwd)
        self.direct[0, p] = self.part(p, x_bwd).astype(jnp.bfloat16)
        self.go(p, 1, self.direct, bwd)

    def second(self, p):
        fwd, bwd, x_fwd, x_bwd = self.place.ways(p)
        mine = self.part(p, x_fwd)
        self.copies[p, 0].wait_recv()
        self.sums[0, p] = (mine + self.relay[1, p].astype(jnp.float32)).astype(jnp.bfloat16)
        self.go(p, 2, self.sums, fwd)

    def own(self, p):
        self.acc[p] = self.part(p, self.place.x)

    def third(self, p):
        self.copies[p, 1].wait_recv()
        self.copies[p, 2].wait_recv()
        self.acc[p] = (
            self.acc[p]
            + self.direct[1, p].astype(jnp.float32)
            + self.sums[1, p].astype(jnp.float32)
        )
        half = self.width // 2
        other = pl.ds(pl.multiple_of((1 - self.place.z) * half, half), half)
        self.zbuf[0, p] = self.acc[p, :, other].astype(jnp.bfloat16)
        self.go(p, 3, self.zbuf, self.place.partner)

    def last(self, p):
        self.copies[p, 3].wait_recv()
        half = self.width // 2
        kept = pl.ds(pl.multiple_of(self.place.z * half, half), half)
        return self.acc[p, :, kept] + self.zbuf[1, p].astype(jnp.float32)

    def finish(self):
        for copy in self.copies.values():
            copy.wait_send()


class Gather:
    def __init__(self, place, whole, sems):
        self.place, self.whole, self.sems = place, whole, sems
        self.rows = whole.shape[0] // PIECES
        self.width = whole.shape[1] // 8
        self.copies = {}

    def view(self, p, head, count):
        width = self.width
        cols = pl.ds(pl.multiple_of(head * width, width), count * width)
        return self.whole.at[p * self.rows : (p + 1) * self.rows, cols]

    def go(self, p, kind, head, count, device):
        view = self.view(p, head, count)
        self.copies[p, kind] = send(view, view, self.sems, p * 6 + kind, device)

    def first(self, p):
        fwd, bwd, x_fwd, x_bwd = self.place.ways(p)
        self.go(p, 0, self.place.me, 1, self.place.partner)
        self.go(p, 1, self.place.me, 1, fwd)
        self.go(p, 2, self.place.me, 1, bwd)

    def second(self, p):
        fwd, bwd, x_fwd, x_bwd = self.place.ways(p)
        self.copies[p, 0].wait_recv()
        mate = self.place.x * 2 + 1 - self.place.z
        self.go(p, 3, mate, 1, fwd)
        self.go(p, 4, mate, 1, bwd)

    def third(self, p):
        fwd, bwd, x_fwd, x_bwd = self.place.ways(p)
        self.copies[p, 1].wait_recv()
        self.copies[p, 3].wait_recv()
        self.go(p, 5, x_bwd * 2, 2, fwd)

    def last(self, p):
        self.copies[p, 2].wait_recv()
        self.copies[p, 4].wait_recv()
        self.copies[p, 5].wait_recv()

    def finish(self):
        for copy in self.copies.values():
            copy.wait_send()


def tail_kernel(
    heads,
    seqs,
    att_ref,
    w_mix_hbm,
    frames_hbm,
    taps_ref,
    bias_ref,
    gain_ref,
    up_hbm,
    down_hbm,
    out_ref,
    w_mix,
    up,
    down,
    resid,
    stream,
    halo,
    pad,
    second,
    whole,
    hidden,
    relay_f,
    direct_f,
    sums_f,
    z_f,
    acc_f,
    ret_in,
    joined,
    local_sems,
    sems_r,
    sems_o,
    sems_h,
    sems_g,
    sems_f,
):
    place = Place(heads, seqs)
    frame_rows, width = out_ref.shape
    rows = frame_rows // PIECES
    own_cols = pl.ds(pl.multiple_of(place.me * width, width), width)
    get_resid = pltpu.make_async_copy(frames_hbm.at[:, own_cols], resid, local_sems.at[0])
    get_up = pltpu.make_async_copy(up_hbm, up, local_sems.at[1])
    get_down = pltpu.make_async_copy(down_hbm, down, local_sems.at[2])
    get_mix = pltpu.make_async_copy(w_mix_hbm, w_mix, local_sems.at[4])
    get_mix.start()
    get_resid.start()
    get_up.start()
    get_down.start()
    place.greet()

    share = att_ref.shape[1] // 2
    back = {}
    for h in (0, 1):
        at = slice(h * share, (h + 1) * share)
        for d in (1, 3, 2):
            back[d, h] = send(
                att_ref.at[lax.rem(place.y + d, YS), at, :],
                ret_in.at[place.y, at, :],
                sems_r,
                h * YS + d,
                place.far(d),
            )
    own_back = pltpu.make_async_copy(
        att_ref.at[place.y], ret_in.at[place.y], local_sems.at[3]
    )
    own_back.start()
    half = frame_rows // 2
    low = lax.broadcasted_iota(jnp.int32, (share, 2 * HD), 1) < HD
    mix = Gather(place, joined, sems_o)
    order = ORDER
    ahead_rows = {0: (0, 2), 1: (1, 3)}
    own_back.wait()
    for h in (0, 1):
        for d in (1, 3, 2):
            back[d, h].wait_recv()
        at = slice(h * share, (h + 1) * share)
        later = slice(half + h * share, half + (h + 1) * share)
        for pair in range(YS // 2):
            cols = pl.ds(pl.multiple_of(place.me * width + pair * 2 * HD, 2 * HD), 2 * HD)
            one = ret_in[2 * pair, at, :].astype(jnp.float32)
            two = ret_in[2 * pair + 1, at, :].astype(jnp.float32)
            joined[at, cols] = jnp.where(low, one, swap(two)).astype(jnp.bfloat16)
            joined[later, cols] = jnp.where(low, swap(one), two).astype(jnp.bfloat16)
        for p in ahead_rows[h]:
            mix.first(p)
    for p in order:
        mix.second(p)
    for p in order:
        mix.third(p)
    get_resid.wait()
    get_mix.wait()

    def place_stream(p):
        at = slice(p * rows, (p + 1) * rows)
        mix.last(p)
        mixed = jnp.dot(joined[at, :], w_mix[...], preferred_element_type=jnp.float32)
        value = (resid[at, :].astype(jnp.float32) + mixed).astype(jnp.bfloat16)
        stream[at, :] = value
        pad[HALO + p * rows : HALO + (p + 1) * rows, :] = value.astype(jnp.float32)

    for p in order:
        place_stream(p)
        if p == 0:
            to_before = send(stream.at[0:HALO, :], halo.at[1], sems_h, 0, place.before)
        if p == PIECES - 1:
            to_after = send(
                stream.at[frame_rows - HALO : frame_rows, :], halo.at[0], sems_h, 1, place.after
            )
    ring = Gather(place, whole, sems_g)

    def convolve(p):
        shift = HALO - KERNEL // 2
        total = jnp.zeros((rows, width), jnp.float32)
        for tap in range(KERNEL):
            total = total + taps_ref[tap : tap + 1, :] * pad[
                pl.ds(p * rows + tap + shift, rows), :
            ]
        at = slice(p * rows, (p + 1) * rows)
        value = pad[HALO + p * rows : HALO + (p + 1) * rows, :] + silu(total + bias_ref[...])
        value = value.astype(jnp.bfloat16)
        second[at, :] = value
        whole[at, own_cols] = value

    def feed(p):
        at = slice(p * rows, (p + 1) * rows)
        cells = whole[at, :].astype(jnp.float32)
        mean = jnp.mean(cells, axis=1, keepdims=True)
        centered = cells - mean
        var = jnp.mean(centered * centered, axis=1, keepdims=True)
        normed = (centered * lax.rsqrt(var + 1e-05) * gain_ref[...]).astype(jnp.bfloat16)
        upper = jnp.dot(normed, up[...], preferred_element_type=jnp.float32)
        hidden[at, :] = silu(upper).astype(jnp.bfloat16)

    order = INSIDE + EDGES
    for p in INSIDE:
        convolve(p)
        ring.first(p)
    to_before.wait_recv()
    to_after.wait_recv()
    top = jnp.where(place.s == 0, 0.0, 1.0)
    bottom = jnp.where(place.s == seqs - 1, 0.0, 1.0)
    pad[0:HALO, :] = halo[0].astype(jnp.float32) * top
    pad[HALO + frame_rows : 2 * HALO + frame_rows, :] = halo[1].astype(jnp.float32) * bottom

    for p in EDGES:
        convolve(p)
        ring.first(p)
    for p in order:
        ring.second(p)
    ahead = 2 * LAG
    for p in order[:ahead]:
        ring.third(p)
    get_up.wait()
    get_down.wait()
    ffn = Scatter(place, hidden, down, (relay_f, direct_f, sums_f, z_f, acc_f), sems_f)
    for i, p in enumerate(order):
        if i + ahead < PIECES:
            ring.third(order[i + ahead])
        ring.last(p)
        feed(p)
        ffn.first(p)
        if i >= LAG:
            ffn.second(order[i - LAG])
        ffn.own(p)
        if i >= 2 * LAG:
            ffn.third(order[i - 2 * LAG])
    for p in order[PIECES - LAG :]:
        ffn.second(p)
    for p in order[PIECES - 2 * LAG :]:
        ffn.third(p)
    for p in order:
        at = slice(p * rows, (p + 1) * rows)
        out_ref[at, :] = (second[at, :].astype(jnp.float32) + ffn.last(p)).astype(out_ref.dtype)
    for copy in back.values():
        copy.wait_send()
    mix.finish()
    to_before.wait_send()
    to_after.wait_send()
    ring.finish()
    ffn.finish()


def tail(attended, w_mix, frames, taps, bias, gain, w_up, w_down):
    width = w_mix.shape[1]
    frame_rows, depth = frames.shape
    hidden = w_up.shape[1]
    rows = frame_rows // PIECES
    vmem = pl.BlockSpec(memory_space=pltpu.VMEM)
    hbm = pl.BlockSpec(memory_space=pltpu.HBM)
    free = pl.BlockSpec(memory_space=pl.ANY)
    bf16, f32 = jnp.bfloat16, jnp.float32
    quarter = depth // 4
    buffers = [pltpu.VMEM((2, PIECES, rows, quarter), bf16)] * 3 + [
        pltpu.VMEM((2, PIECES, rows, width), bf16),
        pltpu.VMEM((PIECES, rows, quarter), f32),
    ]
    dma = pltpu.SemaphoreType.DMA
    return pl.pallas_call(
        functools.partial(tail_kernel, lax.axis_size("head"), lax.axis_size("seq")),
        in_specs=[free, hbm, hbm, vmem, vmem, vmem, hbm, hbm],
        out_specs=vmem,
        out_shape=jax.ShapeDtypeStruct((frame_rows, width), bf16),
        scratch_shapes=[
            pltpu.VMEM((depth, width), bf16),
            pltpu.VMEM((depth, hidden), bf16),
            pltpu.VMEM((hidden, depth), bf16),
            pltpu.VMEM((frame_rows, width), bf16),
            pltpu.VMEM((frame_rows, width), bf16),
            pltpu.VMEM((2, HALO, width), bf16),
            pltpu.VMEM((frame_rows + 2 * HALO, width), f32),
            pltpu.VMEM((frame_rows, width), bf16),
            pltpu.VMEM((frame_rows, depth), bf16),
            pltpu.VMEM((frame_rows, hidden), bf16),
        ]
        + buffers
        + [
            pltpu.VMEM((YS, frame_rows // 2, 2 * HD), bf16),
            pltpu.VMEM((frame_rows, depth), bf16),
            dma((5,)),
            dma((2, 2 * YS)),
            dma((2, PIECES * 6)),
            dma((2, 2)),
            dma((2, PIECES * 6)),
            dma((2, PIECES * 4)),
        ],
        compiler_params=pltpu.CompilerParams(
            collective_id=0, has_side_effects=True, vmem_limit_bytes=LIMIT
        ),
        name="tail",
    )(attended, w_mix, frames, taps, bias[None, :], gain[None, :], w_up, w_down)


def on_device(
    frames,
    w_query,
    w_key,
    w_value,
    w_out,
    conv_taps,
    conv_bias,
    norm_gain,
    w_up,
    w_down,
    block_lists,
    block_counts,
):
    kv_all, q_all, tables, w_mix = front(
        frames, w_query, w_key, w_value, w_out, block_lists, block_counts
    )
    attended = attend_listed(tables, q_all, kv_all)
    return tail(attended, w_mix, frames, conv_taps, conv_bias, norm_gain, w_up, w_down)


def solution(mesh):
    placed = (
        P("seq", None),
        P(None, "head"),
        P(None, "head"),
        P(None, "head"),
        P("head", None),
        P(None, "head"),
        P("head"),
        P(),
        P(None, "head"),
        P("head", None),
        P("seq", None),
        P("seq"),
    )
    return jax.shard_map(
        on_device, mesh=mesh, in_specs=placed, out_specs=P("seq", "head"), check_vma=False
    )
```

```python
import functools

import jax
import jax.numpy as jnp
from jax import lax
from jax.experimental import pallas as pl
from jax.experimental.pallas import tpu as pltpu
from jax.sharding import PartitionSpec as P

HD = 64
KERNEL = 31
NEG = -1e30


MESH = pl.DeviceIdType.MESH
PIECES = 4
LAG = PIECES // 4
ORDER = (0, 2, 1, 3)
INSIDE, EDGES = (1, 2), (0, 3)
HALO = 16
YS = 4
BLOCK = 128
SLOTS = 8
COUNT_ROW = 4
FRONT_LIMIT = 66322432
LIMIT = 66322432


def silu(v):
    return v / (1.0 + jnp.exp(-v))


class Place:
    def __init__(self, heads, seqs):
        self.me = lax.axis_index("head")
        ring = heads // 2
        self.x = lax.div(self.me, 2)
        self.z = lax.rem(self.me, 2)
        self.x_right = lax.rem(self.x + 1, ring)
        self.x_left = lax.rem(self.x + ring - 1, ring)
        self.x_far = lax.rem(self.x + 2, ring)
        self.right = {"head": self.x_right * 2 + self.z}
        self.left = {"head": self.x_left * 2 + self.z}
        self.partner = {"head": self.x * 2 + 1 - self.z}
        self.s = lax.axis_index("seq")
        self.core = lax.rem(self.s, 2)
        self.y = lax.rem(lax.div(self.s, 2), YS)
        self.zl = lax.div(self.s, 2 * YS)
        self.after = {"seq": lax.rem(self.s + 1, seqs)}
        self.before = {"seq": lax.rem(self.s + seqs - 1, seqs)}

    def greet(self):
        barrier = pltpu.get_barrier_semaphore()
        others = [self.right, self.left, self.partner, self.after, self.before]
        others += [self.far(d) for d in range(1, YS)]
        for other in others:
            pl.semaphore_signal(barrier, inc=1, device_id=other, device_id_type=MESH)
        pl.semaphore_wait(barrier, len(others))

    def seq_of(self, z_at, y_at, core_at):
        return (z_at * YS + y_at) * 2 + core_at

    def far(self, d):
        return {"seq": self.seq_of(self.zl, lax.rem(self.y + d, YS), self.core)}

    def ways(self, p):
        if p < PIECES // 2:
            return self.right, self.left, self.x_right, self.x_left
        return self.left, self.right, self.x_left, self.x_right


def send(src, dst, sems, key, device):
    copy = pltpu.make_async_remote_copy(
        src_ref=src,
        dst_ref=dst,
        send_sem=sems.at[0, key],
        recv_sem=sems.at[1, key],
        device_id=device,
        device_id_type=MESH,
    )
    copy.start()
    return copy


def swap(value):
    return pltpu.roll(value, HD, 1)


def front_kernel(
    frames_hbm,
    wq_hbm,
    wk_hbm,
    wv_hbm,
    w_out_hbm,
    lists_ref,
    counts_ref,
    kv_all,
    q_all,
    tables,
    w_mix,
    table,
    x,
    wq,
    wk,
    wv,
    kv_out,
    q_out,
    local_sems,
    sems,
    sems_w,
):
    frame_rows = x.shape[0]
    half = frame_rows // 2
    f32, bf16 = jnp.float32, jnp.bfloat16
    loads = []
    for i, (src, dst) in enumerate(
        ((frames_hbm, x), (wk_hbm, wk), (wv_hbm, wv), (wq_hbm, wq))
    ):
        load = pltpu.make_async_copy(src, dst, local_sems.at[i])
        load.start()
        loads.append(load)

    table[...] = jnp.zeros_like(table)
    table[: lists_ref.shape[0], : lists_ref.shape[1]] = lists_ref[...]
    table[COUNT_ROW : COUNT_ROW + 1, : counts_ref.shape[1]] = counts_ref[...]

    s = lax.axis_index("seq")
    core = lax.rem(s, 2)
    y = lax.rem(lax.div(s, 2), YS)
    zl = lax.div(s, 2 * YS)

    def seq_of(z_at, y_at, core_at):
        return (z_at * YS + y_at) * 2 + core_at

    def far(d):
        return {"seq": seq_of(zl, lax.rem(y + d, YS), core)}

    mate = {"seq": seq_of(zl, y, 1 - core)}
    across = {"seq": seq_of(1 - zl, y, core)}
    barrier = pltpu.get_barrier_semaphore()
    head = lax.axis_index("head")
    heads = w_mix.shape[0] // w_mix.shape[1]

    def head_at(d):
        return lax.rem(head + d, heads)

    others = [far(d) for d in range(1, YS)] + [mate, across]
    others += [{"head": head_at(d)} for d in range(1, heads)]
    for other in others:
        pl.semaphore_signal(barrier, inc=1, device_id=other, device_id_type=MESH)
    width = w_mix.shape[1]
    share = width // 2

    def mix_rows(t):
        start = pl.multiple_of(t * width + core * share, share)
        return w_mix.at[pl.ds(start, share), :]

    def w_cols(t):
        return pl.ds(pl.multiple_of(t * width, width), width)

    low = lax.broadcasted_iota(jnp.int32, (half, 2 * HD), 1) < HD
    for load in loads[:3]:
        load.wait()
    for part in range(2):
        rows = slice(part * half, (part + 1) * half)
        k = jnp.dot(x[rows, :], wk[...], preferred_element_type=f32)
        v = jnp.dot(x[rows, :], wv[...], preferred_element_type=f32)
        for pair in range(YS // 2):
            cols = slice(pair * 2 * HD, (pair + 1) * 2 * HD)
            kp, vp = k[:, cols], v[:, cols]
            kv_out[2 * pair, rows, :] = jnp.where(low, kp, swap(vp)).astype(bf16)
            kv_out[2 * pair + 1, rows, :] = jnp.where(low, swap(kp), vp).astype(bf16)

    def rows_of(z_at, y_at, core_at):
        start = seq_of(z_at, y_at, core_at) * frame_rows
        return kv_all.at[pl.ds(pl.multiple_of(start, frame_rows), frame_rows), :]

    pl.semaphore_wait(barrier, len(others))
    sent = {}
    here = rows_of(zl, y, core)
    sent["across", 0] = send(kv_out.at[y], here, sems, 8, across)
    for d in (1, 3, 2):
        to = lax.rem(y + d, YS)
        sent["kv", d] = send(kv_out.at[to], here, sems, d, far(d))
        sent["table", d] = send(table, tables.at[y], sems, 4 + d, far(d))
    sent["mate", 0] = send(kv_out.at[y], here, sems, 12, mate)
    for d in (3, 5, 4, 1, 7, 2, 6):
        mine = w_out_hbm.at[pl.ds(pl.multiple_of(core * share, share), share), w_cols(head_at(d))]
        sent["w", d] = send(mine, mix_rows(head), sems_w, d, {"head": head_at(d)})
    own_mix = pltpu.make_async_copy(
        w_out_hbm.at[:, w_cols(head)], w_mix.at[w_cols(head), :], local_sems.at[7]
    )
    own_mix.start()

    keep = [
        pltpu.make_async_copy(kv_out.at[y], here, local_sems.at[4]),
        pltpu.make_async_copy(table, tables.at[y], local_sems.at[5]),
    ]
    for copy in keep:
        copy.start()

    loads[3].wait()
    q = 0.125 * jnp.dot(x[...], wq[...], preferred_element_type=f32)
    for pair in range(YS // 2):
        cols = slice(pair * 2 * HD, (pair + 1) * 2 * HD)
        top, bottom = q[:half, cols], q[half:, cols]
        q_out[2 * pair] = jnp.where(low, top, swap(bottom)).astype(bf16)
        q_out[2 * pair + 1] = jnp.where(low, swap(top), bottom).astype(bf16)
    for d in (2, 1, 3):
        to = lax.rem(y + d, YS)
        sent["q", d] = send(q_out.at[to], q_all.at[y], sems, 20 + d, far(d))
    keep.append(pltpu.make_async_copy(q_out.at[y], q_all.at[y], local_sems.at[6]))
    keep[-1].start()

    for d in (1, 3, 2):
        sent["kv", d].wait_recv()
        piece = rows_of(zl, lax.rem(y + YS - d, YS), core)
        sent["across", d] = send(piece, piece, sems, 8 + d, across)
        sent["mate", d] = send(piece, piece, sems, 12 + d, mate)
    for d in (0, 1, 3, 2):
        sent["across", d].wait_recv()
        piece = rows_of(1 - zl, lax.rem(y + YS - d, YS), core)
        sent["over", d] = send(piece, piece, sems, 16 + d, mate)
    for d in range(1, heads):
        sent["w", d].wait_recv()
        piece = mix_rows(head_at(heads - d))
        sent["w_mate", d] = send(piece, piece, sems_w, heads + d, mate)
    for d in range(1, YS):
        sent["table", d].wait_recv()
    for d in range(1, YS):
        sent["q", d].wait_recv()
    for d in range(YS):
        sent["mate", d].wait_recv()
    for d in range(YS):
        sent["over", d].wait_recv()
    for d in range(1, heads):
        sent["w_mate", d].wait_recv()
    own_mix.wait()
    for copy in keep:
        copy.wait()
    for copy in sent.values():
        copy.wait_send()


def attention_kernel(tables_ref, q_ref, kv_ref, out_ref):
    f32, bf16 = jnp.float32, jnp.bfloat16
    sources, half, lanes = q_ref.shape
    block, slots = BLOCK, SLOTS
    per_half = half // block
    low = lax.broadcasted_iota(jnp.int32, (block, lanes), 1) < HD
    slot_col = lax.broadcasted_iota(jnp.int32, (block, slots * block), 1)

    def attend(source, b):
        packed = q_ref[source, (b % per_half) * block : (b % per_half + 1) * block, :]
        packed = packed.astype(f32)
        if b >= per_half:
            packed = swap(packed)
        query = jnp.where(low, packed, 0.0).astype(bf16)
        cells = []
        for j in range(slots):
            start = pl.multiple_of(tables_ref[source, b, j] * block, block)
            cells.append(kv_ref[pl.ds(start, block), :])
        kv = jnp.concatenate(cells, axis=0)
        scores = lax.dot_general(query, kv, (((1,), (1,)), ((), ())), preferred_element_type=f32)
        live = slot_col < tables_ref[source, COUNT_ROW, b] * block
        scores = jnp.where(live, scores, NEG)
        top = jnp.max(scores, axis=1, keepdims=True)
        p = jnp.exp(scores - top)
        total = jnp.sum(p, axis=1, keepdims=True)
        return jnp.dot(p.astype(bf16), kv, preferred_element_type=f32) / total

    for source in range(sources):
        for b in range(per_half):
            early, late = attend(source, b), attend(source, b + per_half)
            rows = slice(b * block, (b + 1) * block)
            out_ref[source, rows, :] = jnp.where(low, swap(early), late).astype(bf16)


def attend_listed(tables, q_all, kv_all):
    vmem = pl.BlockSpec(memory_space=pltpu.VMEM)
    return pl.pallas_call(
        attention_kernel,
        in_specs=[pl.BlockSpec(memory_space=pltpu.SMEM), vmem, vmem],
        out_specs=vmem,
        out_shape=jax.ShapeDtypeStruct(q_all.shape, jnp.bfloat16),
        compiler_params=pltpu.CompilerParams(vmem_limit_bytes=LIMIT),
        name="attend",
    )(tables, q_all, kv_all)


def front(frames, w_query, w_key, w_value, w_out, lists, counts):
    frame_rows, depth = frames.shape
    width = w_query.shape[1]
    seqs = lax.axis_size("seq")
    bf16 = jnp.bfloat16
    hbm = pl.BlockSpec(memory_space=pltpu.HBM)
    free = pl.BlockSpec(memory_space=pl.ANY)
    vmem = pl.BlockSpec(memory_space=pltpu.VMEM)
    dma = pltpu.SemaphoreType.DMA
    lanes = 2 * HD
    return pl.pallas_call(
        front_kernel,
        in_specs=[hbm, hbm, hbm, hbm, hbm, vmem, vmem],
        out_specs=[free, free, free, free],
        out_shape=[
            jax.ShapeDtypeStruct((seqs * frame_rows, lanes), bf16),
            jax.ShapeDtypeStruct((YS, frame_rows // 2, lanes), bf16),
            jax.ShapeDtypeStruct((YS, 8, 128), jnp.int32),
            jax.ShapeDtypeStruct((depth, width), bf16),
        ],
        scratch_shapes=[
            pltpu.VMEM((8, 128), jnp.int32),
            pltpu.VMEM((frame_rows, depth), bf16),
            pltpu.VMEM((depth, width), bf16),
            pltpu.VMEM((depth, width), bf16),
            pltpu.VMEM((depth, width), bf16),
            pltpu.VMEM((YS, frame_rows, lanes), bf16),
            pltpu.VMEM((YS, frame_rows // 2, lanes), bf16),
            dma((8,)),
            dma((2, 24)),
            dma((2, 16)),
        ],
        compiler_params=pltpu.CompilerParams(
            collective_id=1, has_side_effects=True, vmem_limit_bytes=FRONT_LIMIT
        ),
        name="front",
    )(frames, w_query, w_key, w_value, w_out, lists, counts[None, :])


class Scatter:
    def __init__(self, place, a, w, bufs, sems):
        self.place, self.a, self.w = place, a, w
        (self.relay, self.direct, self.sums, self.zbuf, self.acc) = bufs
        self.sems = sems
        self.rows = a.shape[0] // PIECES
        self.width = w.shape[1] // 4
        self.copies = {}

    def part(self, p, xd):
        cols = pl.ds(pl.multiple_of(xd * self.width, self.width), self.width)
        return jnp.dot(
            self.a[p * self.rows : (p + 1) * self.rows, :],
            self.w[:, cols],
            preferred_element_type=jnp.float32,
        )

    def go(self, p, kind, buf, device):
        self.copies[p, kind] = send(
            buf.at[0, p], buf.at[1, p], self.sems, p * 4 + kind, device
        )

    def first(self, p):
        fwd, bwd, x_fwd, x_bwd = self.place.ways(p)
        self.relay[0, p] = self.part(p, self.place.x_far).astype(jnp.bfloat16)
        self.go(p, 0, self.relay, fwd)
        self.direct[0, p] = self.part(p, x_bwd).astype(jnp.bfloat16)
        self.go(p, 1, self.direct, bwd)

    def second(self, p):
        fwd, bwd, x_fwd, x_bwd = self.place.ways(p)
        mine = self.part(p, x_fwd)
        self.copies[p, 0].wait_recv()
        self.sums[0, p] = (mine + self.relay[1, p].astype(jnp.float32)).astype(jnp.bfloat16)
        self.go(p, 2, self.sums, fwd)

    def own(self, p):
        self.acc[p] = self.part(p, self.place.x)

    def third(self, p):
        self.copies[p, 1].wait_recv()
        self.copies[p, 2].wait_recv()
        self.acc[p] = (
            self.acc[p]
            + self.direct[1, p].astype(jnp.float32)
            + self.sums[1, p].astype(jnp.float32)
        )
        half = self.width // 2
        other = pl.ds(pl.multiple_of((1 - self.place.z) * half, half), half)
        self.zbuf[0, p] = self.acc[p, :, other].astype(jnp.bfloat16)
        self.go(p, 3, self.zbuf, self.place.partner)

    def last(self, p):
        self.copies[p, 3].wait_recv()
        half = self.width // 2
        kept = pl.ds(pl.multiple_of(self.place.z * half, half), half)
        return self.acc[p, :, kept] + self.zbuf[1, p].astype(jnp.float32)

    def finish(self):
        for copy in self.copies.values():
            copy.wait_send()


class Gather:
    def __init__(self, place, whole, sems):
        self.place, self.whole, self.sems = place, whole, sems
        self.rows = whole.shape[0] // PIECES
        self.width = whole.shape[1] // 8
        self.copies = {}

    def view(self, p, head, count):
        width = self.width
        cols = pl.ds(pl.multiple_of(head * width, width), count * width)
        return self.whole.at[p * self.rows : (p + 1) * self.rows, cols]

    def go(self, p, kind, head, count, device):
        view = self.view(p, head, count)
        self.copies[p, kind] = send(view, view, self.sems, p * 6 + kind, device)

    def first(self, p):
        fwd, bwd, x_fwd, x_bwd = self.place.ways(p)
        self.go(p, 0, self.place.me, 1, self.place.partner)
        self.go(p, 1, self.place.me, 1, fwd)
        self.go(p, 2, self.place.me, 1, bwd)

    def second(self, p):
        fwd, bwd, x_fwd, x_bwd = self.place.ways(p)
        self.copies[p, 0].wait_recv()
        mate = self.place.x * 2 + 1 - self.place.z
        self.go(p, 3, mate, 1, fwd)
        self.go(p, 4, mate, 1, bwd)

    def third(self, p):
        fwd, bwd, x_fwd, x_bwd = self.place.ways(p)
        self.copies[p, 1].wait_recv()
        self.copies[p, 3].wait_recv()
        self.go(p, 5, x_bwd * 2, 2, fwd)

    def last(self, p):
        self.copies[p, 2].wait_recv()
        self.copies[p, 4].wait_recv()
        self.copies[p, 5].wait_recv()

    def finish(self):
        for copy in self.copies.values():
            copy.wait_send()


def tail_kernel(
    heads,
    seqs,
    att_ref,
    w_mix_hbm,
    frames_hbm,
    taps_ref,
    bias_ref,
    gain_ref,
    up_hbm,
    down_hbm,
    out_ref,
    w_mix,
    up,
    down,
    resid,
    stream,
    halo,
    pad,
    second,
    whole,
    hidden,
    relay_f,
    direct_f,
    sums_f,
    z_f,
    acc_f,
    ret_in,
    joined,
    local_sems,
    sems_r,
    sems_o,
    sems_h,
    sems_g,
    sems_f,
):
    place = Place(heads, seqs)
    frame_rows, width = out_ref.shape
    rows = frame_rows // PIECES
    own_cols = pl.ds(pl.multiple_of(place.me * width, width), width)
    get_resid = pltpu.make_async_copy(frames_hbm.at[:, own_cols], resid, local_sems.at[0])
    get_up = pltpu.make_async_copy(up_hbm, up, local_sems.at[1])
    get_down = pltpu.make_async_copy(down_hbm, down, local_sems.at[2])
    get_mix = pltpu.make_async_copy(w_mix_hbm, w_mix, local_sems.at[4])
    get_mix.start()
    get_resid.start()
    get_up.start()
    get_down.start()
    place.greet()

    share = att_ref.shape[1] // 2
    back = {}
    for h in (0, 1):
        at = slice(h * share, (h + 1) * share)
        for d in (1, 3, 2):
            back[d, h] = send(
                att_ref.at[lax.rem(place.y + d, YS), at, :],
                ret_in.at[place.y, at, :],
                sems_r,
                h * YS + d,
                place.far(d),
            )
    own_back = pltpu.make_async_copy(
        att_ref.at[place.y], ret_in.at[place.y], local_sems.at[3]
    )
    own_back.start()
    half = frame_rows // 2
    low = lax.broadcasted_iota(jnp.int32, (share, 2 * HD), 1) < HD
    mix = Gather(place, joined, sems_o)
    order = ORDER
    ahead_rows = {0: (0, 2), 1: (1, 3)}
    own_back.wait()
    for h in (0, 1):
        for d in (1, 3, 2):
            back[d, h].wait_recv()
        at = slice(h * share, (h + 1) * share)
        later = slice(half + h * share, half + (h + 1) * share)
        for pair in range(YS // 2):
            cols = pl.ds(pl.multiple_of(place.me * width + pair * 2 * HD, 2 * HD), 2 * HD)
            one = ret_in[2 * pair, at, :].astype(jnp.float32)
            two = ret_in[2 * pair + 1, at, :].astype(jnp.float32)
            joined[at, cols] = jnp.where(low, one, swap(two)).astype(jnp.bfloat16)
            joined[later, cols] = jnp.where(low, swap(one), two).astype(jnp.bfloat16)
        for p in ahead_rows[h]:
            mix.first(p)
    for p in order:
        mix.second(p)
    for p in order:
        mix.third(p)
    get_resid.wait()
    get_mix.wait()

    def place_stream(p):
        at = slice(p * rows, (p + 1) * rows)
        mix.last(p)
        mixed = jnp.dot(joined[at, :], w_mix[...], preferred_element_type=jnp.float32)
        value = (resid[at, :].astype(jnp.float32) + mixed).astype(jnp.bfloat16)
        stream[at, :] = value
        pad[HALO + p * rows : HALO + (p + 1) * rows, :] = value.astype(jnp.float32)

    for p in order:
        place_stream(p)
        if p == 0:
            to_before = send(stream.at[0:HALO, :], halo.at[1], sems_h, 0, place.before)
        if p == PIECES - 1:
            to_after = send(
                stream.at[frame_rows - HALO : frame_rows, :], halo.at[0], sems_h, 1, place.after
            )
    ring = Gather(place, whole, sems_g)

    def convolve(p):
        shift = HALO - KERNEL // 2
        total = jnp.zeros((rows, width), jnp.float32)
        for tap in range(KERNEL):
            total = total + taps_ref[tap : tap + 1, :] * pad[
                pl.ds(p * rows + tap + shift, rows), :
            ]
        at = slice(p * rows, (p + 1) * rows)
        value = pad[HALO + p * rows : HALO + (p + 1) * rows, :] + silu(total + bias_ref[...])
        value = value.astype(jnp.bfloat16)
        second[at, :] = value
        whole[at, own_cols] = value

    def feed(p):
        at = slice(p * rows, (p + 1) * rows)
        cells = whole[at, :].astype(jnp.float32)
        mean = jnp.mean(cells, axis=1, keepdims=True)
        centered = cells - mean
        var = jnp.mean(centered * centered, axis=1, keepdims=True)
        normed = (centered * lax.rsqrt(var + 1e-05) * gain_ref[...]).astype(jnp.bfloat16)
        upper = jnp.dot(normed, up[...], preferred_element_type=jnp.float32)
        hidden[at, :] = silu(upper).astype(jnp.bfloat16)

    order = INSIDE + EDGES
    for p in INSIDE:
        convolve(p)
        ring.first(p)
    to_before.wait_recv()
    to_after.wait_recv()
    top = jnp.where(place.s == 0, 0.0, 1.0)
    bottom = jnp.where(place.s == seqs - 1, 0.0, 1.0)
    pad[0:HALO, :] = halo[0].astype(jnp.float32) * top
    pad[HALO + frame_rows : 2 * HALO + frame_rows, :] = halo[1].astype(jnp.float32) * bottom

    for p in EDGES:
        convolve(p)
        ring.first(p)
    for p in order:
        ring.second(p)
    ahead = 2 * LAG
    for p in order[:ahead]:
        ring.third(p)
    get_up.wait()
    get_down.wait()
    ffn = Scatter(place, hidden, down, (relay_f, direct_f, sums_f, z_f, acc_f), sems_f)
    for i, p in enumerate(order):
        if i + ahead < PIECES:
            ring.third(order[i + ahead])
        ring.last(p)
        feed(p)
        ffn.first(p)
        if i >= LAG:
            ffn.second(order[i - LAG])
        ffn.own(p)
        if 2 * LAG <= i < PIECES - LAG:
            ffn.third(order[i - 2 * LAG])
    for p in order[PIECES - LAG :]:
        ffn.second(p)
    for p in order[PIECES - 3 * LAG :]:
        ffn.third(p)
    for p in order:
        at = slice(p * rows, (p + 1) * rows)
        out_ref[at, :] = (second[at, :].astype(jnp.float32) + ffn.last(p)).astype(out_ref.dtype)
    for copy in back.values():
        copy.wait_send()
    mix.finish()
    to_before.wait_send()
    to_after.wait_send()
    ring.finish()
    ffn.finish()


def tail(attended, w_mix, frames, taps, bias, gain, w_up, w_down):
    width = w_mix.shape[1]
    frame_rows, depth = frames.shape
    hidden = w_up.shape[1]
    rows = frame_rows // PIECES
    vmem = pl.BlockSpec(memory_space=pltpu.VMEM)
    hbm = pl.BlockSpec(memory_space=pltpu.HBM)
    free = pl.BlockSpec(memory_space=pl.ANY)
    bf16, f32 = jnp.bfloat16, jnp.float32
    quarter = depth // 4
    buffers = [pltpu.VMEM((2, PIECES, rows, quarter), bf16)] * 3 + [
        pltpu.VMEM((2, PIECES, rows, width), bf16),
        pltpu.VMEM((PIECES, rows, quarter), f32),
    ]
    dma = pltpu.SemaphoreType.DMA
    return pl.pallas_call(
        functools.partial(tail_kernel, lax.axis_size("head"), lax.axis_size("seq")),
        in_specs=[free, hbm, hbm, vmem, vmem, vmem, hbm, hbm],
        out_specs=vmem,
        out_shape=jax.ShapeDtypeStruct((frame_rows, width), bf16),
        scratch_shapes=[
            pltpu.VMEM((depth, width), bf16),
            pltpu.VMEM((depth, hidden), bf16),
            pltpu.VMEM((hidden, depth), bf16),
            pltpu.VMEM((frame_rows, width), bf16),
            pltpu.VMEM((frame_rows, width), bf16),
            pltpu.VMEM((2, HALO, width), bf16),
            pltpu.VMEM((frame_rows + 2 * HALO, width), f32),
            pltpu.VMEM((frame_rows, width), bf16),
            pltpu.VMEM((frame_rows, depth), bf16),
            pltpu.VMEM((frame_rows, hidden), bf16),
        ]
        + buffers
        + [
            pltpu.VMEM((YS, frame_rows // 2, 2 * HD), bf16),
            pltpu.VMEM((frame_rows, depth), bf16),
            dma((5,)),
            dma((2, 2 * YS)),
            dma((2, PIECES * 6)),
            dma((2, 2)),
            dma((2, PIECES * 6)),
            dma((2, PIECES * 4)),
        ],
        compiler_params=pltpu.CompilerParams(
            collective_id=0, has_side_effects=True, vmem_limit_bytes=LIMIT
        ),
        name="tail",
    )(attended, w_mix, frames, taps, bias[None, :], gain[None, :], w_up, w_down)


def on_device(
    frames,
    w_query,
    w_key,
    w_value,
    w_out,
    conv_taps,
    conv_bias,
    norm_gain,
    w_up,
    w_down,
    block_lists,
    block_counts,
):
    kv_all, q_all, tables, w_mix = front(
        frames, w_query, w_key, w_value, w_out, block_lists, block_counts
    )
    attended = attend_listed(tables, q_all, kv_all)
    return tail(attended, w_mix, frames, conv_taps, conv_bias, norm_gain, w_up, w_down)


def solution(mesh):
    placed = (
        P("seq", None),
        P(None, "head"),
        P(None, "head"),
        P(None, "head"),
        P("head", None),
        P(None, "head"),
        P("head"),
        P(),
        P(None, "head"),
        P("head", None),
        P("seq", None),
        P("seq"),
    )
    return jax.shard_map(
        on_device, mesh=mesh, in_specs=placed, out_specs=P("seq", "head"), check_vma=False
    )
```
